256 devices in a mesh: depth: 64 (over z, x, core), lat: 4 (over y).
Axes of the slice: x: 4, y: 4, z: 8, core: 2. Of those that a mesh axis runs over, the one named last changes fastest.
Arguments:
- phase: float32 [2048, 256, 128], P('depth', 'lat'), may hold values from 0 to 1
- temper: float32 [2048, 256, 128], P('depth', 'lat'), may hold values from -3 to 3
- iface_count: int32 [64, 4], P('depth', 'lat'), may hold values from 1 to 32, as said below
Outputs:
- phase_next: float32 [2048, 256, 128], P('depth', 'lat')
- heat_next: float32 [2048, 256, 128], P('depth', 'lat')
- picture: float32 [4, 256, 512], P(None, 'lat', 'depth')
The draws below stay inside these ranges and needn't reach their ends.
Inputs may be any that keep to these rules, and one draw needn't show every extreme that they name: `iface_count`: per brick a count of 1 to 32; some brick has exactly 32 and another exactly 1.
All inputs are finite; a program needn't handle non-finite values.
Results may differ from the reference program's by a relative error of at most 0.0003.
Values sent between devices are 32-bit elements; how exact they have to be, the bound alone decides.
No kernel may reach another device: no remote copies, remote signals or barrier semaphores. Data moves between devices by JAX's collectives and lax.ppermute only.
A program may use at most 64 MiB of HBM per device.

```python
import math
import jax
import jax.numpy as jnp
import numpy as np
from jax import lax

CX = 32
CY = 64
VIEWS = 4
SWEEPS = 3
NX = 2048
NY = 256
NZ = 128
N_DEPTH = 64
N_LAT = 4


def draw_iface_count(key, part):
    first_key = jax.random.fold_in(key, 11)
    second_key = jax.random.fold_in(key, 12)
    place_key = jax.random.fold_in(key, 13)
    first_draw = jax.random.randint(first_key, (N_DEPTH * N_LAT,), 1, CX + 1)
    second_draw = jax.random.randint(second_key, (N_DEPTH * N_LAT,), 1, CX + 1)
    counts = jnp.minimum(first_draw, second_draw).astype(jnp.int32)
    position = jax.random.randint(place_key, (), 0, N_DEPTH * N_LAT)
    counts = counts.at[position].set(CX)
    counts = counts.at[(position + 1) % (N_DEPTH * N_LAT)].set(1)
    return counts.reshape(N_DEPTH, N_LAT).astype(jnp.int32)


def levels(own_key, dims, shards, least, high):
    def one(dim, shards_of):
        steps = jax.random.uniform(jax.random.fold_in(jax.random.fold_in(own_key, 6), dim), (shards_of,), jnp.float32, least / len(shards), high / len(shards))
        return jnp.repeat(jnp.exp(steps), dims[dim] // shards_of).reshape((-1,) + (1,) * (len(dims) - dim - 1))

    loudness = one(*shards[0])
    for cut in shards[1:]:
        loudness = loudness * one(*cut)
    return loudness


def bell_draw(stream_key, dims, deviation, bound, shards=(), held_as=jnp.bfloat16):
    result = deviation * jax.random.normal(stream_key, dims, jnp.float32)
    if shards:
        result = result * levels(stream_key, dims, shards, -0.22, 0.18)
    return jnp.clip(result, -bound, bound).astype(held_as)


def setup_inputs(seed: int = 0) -> dict:
    key_list = jax.random.split(jax.random.key(seed), 4)
    phase = jnp.clip(1.0 * jax.random.uniform(key_list[0], (NX, NY, NZ), jnp.float32) ** levels(key_list[0], (NX, NY, NZ), ((0, 64), (1, 4)), -0.2, 0.2), 0.0, 1.0)
    temper = bell_draw(key_list[1], (NX, NY, NZ), 0.5, 3.0, ((0, 64), (1, 4)), jnp.float32)
    iface_count = draw_iface_count(jax.random.fold_in(key_list[3], 71), 0)
    return {"phase": phase, "temper": temper, "iface_count": iface_count}


DIFFUSION = (0.5, 2.0)
TIME_STEP = 0.4
COUPLE = 0.6
LATENT = 0.5
SHEAR_Y = (1.6, -1.6, 0.8, -1.2)
SHEAR_Z = (0.9, -0.6, -0.9, 0.3)
CENTERS = (-0.8, 0.0, 0.8)


def thetas(sweep_total):
    chebyshev = []
    for f in range(2):
        highest = 1.0 + 12.0 * DIFFUSION[f]
        entries = [0.5 * (highest + 1.0) + 0.5 * (highest - 1.0) * math.cos((2 * j + 1) * math.pi / (2 * sweep_total)) for j in range(sweep_total)]
        chebyshev.append(entries)
    return np.array(chebyshev)


def stencil(padded):
    summed = padded[:, 2:, 1:-1, 1:-1] + padded[:, :-2, 1:-1, 1:-1]
    summed = summed + padded[:, 1:-1, 2:, 1:-1] + padded[:, 1:-1, :-2, 1:-1]
    summed = summed + padded[:, 1:-1, 1:-1, 2:] + padded[:, 1:-1, 1:-1, :-2]
    return summed


def sources(phase, temper):
    reaction = phase * (1.0 - phase) * (phase - 0.5 + COUPLE * temper)
    return jnp.stack([phase + TIME_STEP * reaction, temper + LATENT * TIME_STEP * reaction])


def relax(current, source, diffusion, step_size, padded):
    applied = current + diffusion * (6.0 * current - stencil(padded))
    return current + (source - applied) / step_size


def offsets(layers, shear):
    offset = shear * np.arange(layers) / layers
    whole_part = np.floor(offset)
    return whole_part.astype(np.int32), offset - whole_part


def footprint(padded, layer_mask, opacity_scale):
    layers = padded.shape[1]
    row_count = padded.shape[2] - 4
    col_count = padded.shape[3] - 2
    layer_ids = jnp.arange(layers).astype(jnp.int32)[:, None]
    pictures = []
    for v in range(len(SHEAR_Y)):
        base_y, frac_y = offsets(layers, SHEAR_Y[v])
        base_z, frac_z = offsets(layers, SHEAR_Z[v])
        row_ids = jnp.asarray(base_y).astype(jnp.int32)[:, None] + 2 + jnp.arange(row_count).astype(jnp.int32)[None, :]
        near_row = padded[:, layer_ids, row_ids, :]
        far_row = padded[:, layer_ids, row_ids + 1, :]
        frac_row = jnp.asarray(frac_y, jnp.float32)[None, :, None, None]
        blended = (1.0 - frac_row) * near_row + frac_row * far_row
        col_ids = jnp.asarray(base_z).astype(jnp.int32)[:, None] + 1 + jnp.arange(col_count).astype(jnp.int32)[None, :]
        col_ids = jnp.broadcast_to(col_ids[None, :, None, :], (2, layers, row_count, col_count))
        near_col = jnp.take_along_axis(blended, col_ids, axis=3)
        far_col = jnp.take_along_axis(blended, col_ids + 1, axis=3)
        frac_col = jnp.asarray(frac_z, jnp.float32)[None, :, None, None]
        sampled = (1.0 - frac_col) * near_col + frac_col * far_col
        thickness = opacity_scale * sampled[0] * sampled[0] * layer_mask[:, :, None]
        optical = jnp.cumsum(thickness, axis=0)
        weight = jnp.exp(-(optical - thickness)) * (1.0 - jnp.exp(-thickness))
        colours = []
        for centre in CENTERS:
            distance = sampled[1] - centre
            colours.append(jnp.sum(weight / (1.0 + distance * distance), axis=0))
        colours.append(jnp.exp(-optical[-1]))
        pictures.append(jnp.stack(colours))
    return jnp.concatenate(pictures, axis=2)


def over_blend(in_front, behind):
    return jnp.concatenate([in_front[:3] + in_front[3:] * behind[:3], in_front[3:] * behind[3:]], axis=0)


def reference(phase, temper, iface_count):
    current = jnp.stack([phase, temper])
    source = sources(phase, temper)
    chebyshev = thetas(SWEEPS)
    diffusion = jnp.asarray(np.array(DIFFUSION), jnp.float32).reshape(2, 1, 1, 1)
    for k in range(SWEEPS):
        padded = jnp.pad(current, ((0, 0), (1, 1), (1, 1), (1, 1)))
        step_size = jnp.asarray(chebyshev[:, k], jnp.float32).reshape(2, 1, 1, 1)
        current = relax(current, source, diffusion, step_size, padded)
    padded_all = jnp.pad(current, ((0, 0), (0, 0), (2, 2), (1, 1)))
    local_layers = jnp.arange(CX).astype(jnp.int32)

    def render_slab(composite, d):
        slab_cells = lax.dynamic_slice_in_dim(padded_all, (d * CX).astype(jnp.int32), CX, 1)
        row_counts = jnp.repeat(iface_count[d], CY)
        layer_mask = (local_layers[:, None] < row_counts[None, :]).astype(jnp.float32)
        picture = footprint(slab_cells, layer_mask, 4.0 / NX)
        return over_blend(composite, picture), None

    start = jnp.concatenate([jnp.zeros((3, NY, VIEWS * NZ), jnp.float32), jnp.ones((1, NY, VIEWS * NZ), jnp.float32)], axis=0)
    composite, unused = lax.scan(render_slab, start, jnp.arange(N_DEPTH).astype(jnp.int32))
    return current[0], current[1], composite
```

```python
import functools
import math

import jax
import jax.numpy as jnp
import numpy as np
from jax import lax
from jax.experimental import pallas as pl
from jax.experimental.pallas import tpu as pltpu
from jax.sharding import PartitionSpec as P

SWEEPS = 3
DIFFUSION = (0.5, 2.0)
TIME_STEP = 0.4
COUPLE = 0.6
LATENT = 0.5
SHEAR_Y = (1.6, -1.6, 0.8, -1.2)
SHEAR_Z = (0.9, -0.6, -0.9, 0.3)
CX, CY, NZ = 32, 64, 128
NX = 2048
VIEWS = 4

HALO = 3
RIM = 5
EX = CX + 2 * HALO
ROW0 = 8
EY = CY + 2 * ROW0
CORNER = 4
RELATIVE = (0, 3, 1, 2)


def thetas(sweep_total):
    chebyshev = []
    for f in range(2):
        highest = 1.0 + 12.0 * DIFFUSION[f]
        entries = [
            0.5 * (highest + 1.0)
            + 0.5 * (highest - 1.0) * math.cos((2 * j + 1) * math.pi / (2 * sweep_total))
            for j in range(sweep_total)
        ]
        chebyshev.append(entries)
    return np.array(chebyshev)


VMEM = pl.BlockSpec(memory_space=pltpu.VMEM)
SMEM = pl.BlockSpec(memory_space=pltpu.SMEM)
ANY = pl.BlockSpec(memory_space=pl.ANY)


def pack_kernel(phase, temper, ext, depth_a, depth_b, lat_a, lat_b, aa, ab, ba, bb, sems):
    copies = []
    for f, field in enumerate((phase, temper)):
        copies.append(
            pltpu.make_async_copy(
                field, ext.at[f, pl.ds(HALO, CX), pl.ds(ROW0, CY), :], sems.at[f]
            )
        )
    for copy in copies:
        copy.start()
    d_odd = lax.rem(lax.axis_index("depth"), 2)
    l_odd = lax.rem(lax.axis_index("lat"), 2)
    layer_a = HALO + (1 - d_odd) * (CX - HALO)
    layer_b = HALO + d_odd * (CX - HALO)
    row_a = ROW0 + (1 - l_odd) * (CY - RIM)
    row_b = ROW0 + l_odd * (CY - RIM)
    corner_a = ROW0 + (1 - l_odd) * (CY - CORNER)
    corner_b = ROW0 + l_odd * (CY - CORNER)
    for f in range(2):
        copies[f].wait()

        def lat_rows(x, carry):
            at = (f * CX + x) * RIM
            lat_a[pl.ds(at, RIM), :] = ext[f, HALO + x, pl.ds(row_a, RIM), :]
            lat_b[pl.ds(at, RIM), :] = ext[f, HALO + x, pl.ds(row_b, RIM), :]
            return carry

        lax.fori_loop(0, CX, lat_rows, 0, unroll=4)
        for k in range(HALO):
            depth_a[f, k] = ext[f, layer_a + k, pl.ds(ROW0, CY), :]
            depth_b[f, k] = ext[f, layer_b + k, pl.ds(ROW0, CY), :]
            at = pl.ds((f * HALO + k) * CORNER, CORNER)
            aa[at, :] = ext[f, layer_a + k, pl.ds(corner_a, CORNER), :]
            ab[at, :] = ext[f, layer_a + k, pl.ds(corner_b, CORNER), :]
            ba[at, :] = ext[f, layer_b + k, pl.ds(corner_a, CORNER), :]
            bb[at, :] = ext[f, layer_b + k, pl.ds(corner_b, CORNER), :]


def pack(phase, temper):
    f32 = jnp.float32
    return pl.pallas_call(
        pack_kernel,
        out_shape=[
            jax.ShapeDtypeStruct((2, EX, EY, NZ), f32),
            jax.ShapeDtypeStruct((2, HALO, CY, NZ), f32),
            jax.ShapeDtypeStruct((2, HALO, CY, NZ), f32),
            jax.ShapeDtypeStruct((2 * CX * RIM, NZ), f32),
            jax.ShapeDtypeStruct((2 * CX * RIM, NZ), f32),
        ]
        + [jax.ShapeDtypeStruct((2 * HALO * CORNER, NZ), f32)] * 4,
        in_specs=[ANY, ANY],
        out_specs=[VMEM] * 9,
        scratch_shapes=[pltpu.SemaphoreType.DMA((2,))],
        compiler_params=pltpu.CompilerParams(vmem_limit_bytes=20 << 20),
    )(phase, temper)


def unpack(ext, depth_a, depth_b, lat_a, lat_b, aa, ab, ba, bb):
    d_odd = lax.rem(lax.axis_index("depth"), 2)
    l_odd = lax.rem(lax.axis_index("lat"), 2)
    layer_a = (1 - d_odd) * (HALO + CX)
    layer_b = d_odd * (HALO + CX)
    row_a = ROW0 - RIM + (1 - l_odd) * (RIM + CY)
    row_b = ROW0 - RIM + l_odd * (RIM + CY)
    corner_a = ROW0 - CORNER + (1 - l_odd) * (CORNER + CY)
    corner_b = ROW0 - CORNER + l_odd * (CORNER + CY)
    for f in range(2):

        def lat_rows(x, carry):
            at = (f * CX + x) * RIM
            ext[f, HALO + x, pl.ds(row_a, RIM), :] = lat_a[pl.ds(at, RIM), :]
            ext[f, HALO + x, pl.ds(row_b, RIM), :] = lat_b[pl.ds(at, RIM), :]
            return carry

        lax.fori_loop(0, CX, lat_rows, 0, unroll=4)
        for k in range(HALO):
            ext[f, layer_a + k, pl.ds(ROW0, CY), :] = depth_a[f, k]
            ext[f, layer_b + k, pl.ds(ROW0, CY), :] = depth_b[f, k]
            at = pl.ds((f * HALO + k) * CORNER, CORNER)
            ext[f, layer_a + k, pl.ds(corner_a, CORNER), :] = aa[at, :]
            ext[f, layer_a + k, pl.ds(corner_b, CORNER), :] = ab[at, :]
            ext[f, layer_b + k, pl.ds(corner_a, CORNER), :] = ba[at, :]
            ext[f, layer_b + k, pl.ds(corner_b, CORNER), :] = bb[at, :]


FIRST_ROW = ROW0 - CORNER
TILES = (CY + 2 * CORNER) // 8


def zero_outside(ref, first, last):
    depth = lax.axis_index("depth")
    lat = lax.axis_index("lat")

    @pl.when(depth == 0)
    def _():
        for f in range(2):
            for x in range(first, HALO):
                ref[f, x] = jnp.zeros((EY, NZ), jnp.float32)

    @pl.when(depth == lax.axis_size("depth") - 1)
    def _():
        for f in range(2):
            for x in range(HALO + CX, last):
                ref[f, x] = jnp.zeros((EY, NZ), jnp.float32)

    def zero_rows(row):
        def layer(x, carry):
            for f in range(2):
                ref[f, x, pl.ds(row, 8), :] = jnp.zeros((8, NZ), jnp.float32)
            return carry

        lax.fori_loop(first, last, layer, 0, unroll=4)

    @pl.when(lat == 0)
    def _():
        zero_rows(0)

    @pl.when(lat == lax.axis_size("lat") - 1)
    def _():
        zero_rows(ROW0 + CY)


def sweep(j, inp, out, source, first, last):
    theta = thetas(SWEEPS)
    lane = lax.broadcasted_iota(jnp.int32, (8, NZ), 1)
    low_edge = lane == 0
    high_edge = lane == NZ - 1

    def layer(x, carry):
        for t in range(TILES):
            row = FIRST_ROW + 8 * t
            centres = [inp[f, x, pl.ds(row, 8), :] for f in range(2)]
            if j == 0:
                p, h = centres
                reaction = TIME_STEP * (p * (1.0 - p) * ((p - 0.5) + COUPLE * h))
                sources = (p + reaction, h + LATENT * reaction)
                for f in range(2):
                    source[f, x, pl.ds(row, 8), :] = sources[f]
            else:
                sources = [source[f, x, pl.ds(row, 8), :] for f in range(2)]
            for f in range(2):
                u = centres[f]
                around = inp[f, x - 1, pl.ds(row, 8), :] + inp[f, x + 1, pl.ds(row, 8), :]
                sides = inp[f, x, pl.ds(row - 1, 8), :] + inp[f, x, pl.ds(row + 1, 8), :]
                below = jnp.where(low_edge, 0.0, pltpu.roll(u, 1, 1))
                above = jnp.where(high_edge, 0.0, pltpu.roll(u, NZ - 1, 1))
                total = (around + sides) + (below + above)
                k = DIFFUSION[f]
                inverse = 1.0 / theta[f, j]
                value = (
                    float(1.0 - (1.0 + 6.0 * k) * inverse) * u
                    + float(k * inverse) * total
                    + float(inverse) * sources[f]
                )
                out[f, x, pl.ds(row, 8), :] = value
        return carry

    lax.fori_loop(first, last, layer, 0)


def render_view(v, field, count, pic):
    lane = lax.broadcasted_iota(jnp.int32, (8, NZ), 1)
    positive = SHEAR_Z[v] > 0
    edge = (lane == NZ - 1) if positive else (lane == 0)
    inside = jnp.where(edge, 0.0, 1.0)
    shift = NZ - 1 if positive else 1
    tiles = CY // 8
    opacity = 4.0 / NX
    zeros = jnp.zeros((8, NZ), jnp.float32)
    ones = jnp.ones((8, NZ), jnp.float32)

    def whole(x):
        base = [math.floor(SHEAR_Y[v] * i / CX) for i in range(CX)]
        value = jnp.int32(base[0])
        for i in range(1, CX):
            if base[i] != base[i - 1]:
                value = value + jnp.where(x >= i, base[i] - base[i - 1], 0)
        return value

    def layer(x, state):
        trans, reds, greens, blues = state
        xf = x.astype(jnp.float32)
        base_y = whole(x)
        frac_y = xf * (SHEAR_Y[v] / CX) - base_y.astype(jnp.float32)
        frac_z = xf * (abs(SHEAR_Z[v]) / CX)
        near_z = 1.0 - frac_z
        far_z = inside * frac_z
        new = ([], [], [], [])
        for t in range(tiles):
            samples = []
            for f in range(2):
                row = ROW0 + 8 * t + base_y
                near = field[f, HALO + x, pl.ds(row, 8), :]
                far = field[f, HALO + x, pl.ds(row + 1, 8), :]
                mixed = near + frac_y * (far - near)
                samples.append(mixed * near_z + pltpu.roll(mixed, shift, 1) * far_z)
            s0, s1 = samples
            passed = trans[t] * jnp.exp(s0 * s0 * (-opacity))
            weight = trans[t] - passed
            square = s1 * s1
            middle = square + 1.0
            slope = 1.6 * s1
            outer = square + 1.64
            low = outer + slope
            high = outer - slope
            both = low * high
            share = weight / (middle * both)
            rest = share * middle
            new[0].append(passed)
            new[1].append(reds[t] + rest * high)
            new[2].append(greens[t] + share * both)
            new[3].append(blues[t] + rest * low)
        return tuple(tuple(n) for n in new)

    start = (ones,) * tiles, (zeros,) * tiles, (zeros,) * tiles, (zeros,) * tiles
    trans, reds, greens, blues = lax.fori_loop(0, count, layer, start)
    for c, channel in enumerate((reds, greens, blues, trans)):
        for t in range(tiles):
            pic[v, c, pl.ds(8 * t, 8), :] = channel[t]


def brick_kernel(
    ext, depth_a, depth_b, lat_a, lat_b, aa, ab, ba, bb, count,
    phase_next, heat_next, keep, send,
    other, source, pic, turned, sems,
):
    unpack(ext, depth_a, depth_b, lat_a, lat_b, aa, ab, ba, bb)
    sweep(0, ext, other, source, 1, EX - 1)
    zero_outside(other, 1, EX - 1)
    sweep(1, other, ext, source, 2, EX - 2)
    zero_outside(ext, 2, EX - 2)
    sweep(2, ext, other, source, HALO, HALO + CX)
    zero_outside(other, HALO, HALO + CX)
    copies = []
    for f, field in enumerate((phase_next, heat_next)):
        copies.append(
            pltpu.make_async_copy(
                other.at[f, pl.ds(HALO, CX), pl.ds(ROW0, CY), :], field, sems.at[f]
            )
        )
    for copy in copies:
        copy.start()
    layer_count = count[0, 0]
    for v in range(VIEWS):
        render_view(v, other, layer_count, pic)
    for v in range(2):
        for c in range(4):
            square = jnp.concatenate([pic[v, c], pltpu.roll(pic[3 - v, c], 64, 1)], axis=0)
            turned[v, c] = square.T
    depth = lax.axis_index("depth")
    my_core = lax.rem(depth, 2)
    my_x = lax.rem(lax.div(depth, 2), 4)
    my_z = lax.div(depth, 8)
    my_class = jnp.where(my_z < 4, my_z, 7 - my_z)
    for core_rel, target in ((0, keep), (1, send)):
        for i, x_rel in enumerate(RELATIVE):
            for j, z_rel in enumerate(RELATIVE):
                group = my_class ^ z_rel
                block = (group & 1) * 8 + (my_x ^ x_rel) * 2 + (my_core ^ core_rel)
                for c in range(4):
                    target[i * 4 + j, c] = turned[
                        group >> 1, c, pl.ds(pl.multiple_of(block * 8, 8), 8), :
                    ]
    for copy in copies:
        copy.wait()


def brick(ext, halos, iface_count):
    f32 = jnp.float32
    pieces = jax.ShapeDtypeStruct((16, 4, 8, NZ), f32)
    return pl.pallas_call(
        brick_kernel,
        out_shape=[
            jax.ShapeDtypeStruct((CX, CY, NZ), f32),
            jax.ShapeDtypeStruct((CX, CY, NZ), f32),
            pieces,
            pieces,
        ],
        in_specs=[VMEM] * 9 + [SMEM],
        out_specs=[ANY, ANY, VMEM, VMEM],
        scratch_shapes=[
            pltpu.VMEM((2, EX, EY, NZ), f32),
            pltpu.VMEM((2, EX, EY, NZ), f32),
            pltpu.VMEM((VIEWS, 4, CY, NZ), f32),
            pltpu.VMEM((2, 4, NZ, 2 * CY), f32),
            pltpu.SemaphoreType.DMA((2,)),
        ],
        compiler_params=pltpu.CompilerParams(vmem_limit_bytes=40 << 20),
    )(ext, *halos, iface_count)


def blend(front, back, write):
    clear = front[:, 3]
    for c in range(3):
        write(c, front[:, c] + clear * back[:, c])
    write(3, clear * back[:, 3])


def combine_kernel(bit, mine, theirs, keep, send):
    half = keep.shape[0]
    in_front = (lax.axis_index("depth") >> bit) & 1 == 0

    def write(c, value):
        keep[:, c] = value[:half]
        send[:, c] = value[half:]

    @pl.when(in_front)
    def _():
        blend(mine, theirs, write)

    @pl.when(jnp.logical_not(in_front))
    def _():
        blend(theirs, mine, write)


def combine(bit, mine, theirs):
    half = jax.ShapeDtypeStruct((mine.shape[0] // 2,) + mine.shape[1:], jnp.float32)
    return pl.pallas_call(
        functools.partial(combine_kernel, bit),
        out_shape=[half, half],
        in_specs=[VMEM] * 2,
        out_specs=[VMEM] * 2,
        compiler_params=pltpu.CompilerParams(vmem_limit_bytes=8 << 20),
    )(mine, theirs)


def last_kernel(bit, mine, theirs, out, mixed):
    low_half = (lax.axis_index("depth") >> bit) & 1 == 0

    def write(c, value):
        mixed[pl.ds(c * 8, 8), :] = value[0]

    @pl.when(low_half)
    def _():
        blend(mine, theirs, write)

    @pl.when(jnp.logical_not(low_half))
    def _():
        blend(theirs, mine, write)

    value = mixed[...]
    value = jnp.where(low_half, value, pltpu.roll(value, 64, 1))
    turned = value.T
    for c in range(4):
        out[c] = turned[:CY, c * 8 : c * 8 + 8]


def last(bit, mine, theirs):
    return pl.pallas_call(
        functools.partial(last_kernel, bit),
        out_shape=jax.ShapeDtypeStruct((4, CY, 8), jnp.float32),
        in_specs=[VMEM] * 2,
        out_specs=VMEM,
        scratch_shapes=[pltpu.VMEM((128, NZ), jnp.float32)],
        compiler_params=pltpu.CompilerParams(vmem_limit_bytes=8 << 20),
    )(mine, theirs)


def pairs(count, odd):
    result = []
    for i in range(odd, count - 1, 2):
        result += [(i, i + 1), (i + 1, i)]
    return result


def per_device(phase, temper, iface_count):
    depth_size = lax.axis_size("depth")
    lat_size = lax.axis_size("lat")
    ext, *sent = pack(phase, temper)
    depth_pairs = [pairs(depth_size, odd) for odd in range(2)]
    lat_pairs = [pairs(lat_size, odd) for odd in range(2)]
    lat_halo = [lax.ppermute(sent[2 + i], "lat", lat_pairs[i]) for i in range(2)]
    depth_halo = [lax.ppermute(sent[i], "depth", depth_pairs[i]) for i in range(2)]
    corners = []
    for i in range(2):
        for j in range(2):
            both = [
                (a * lat_size + m, b * lat_size + n)
                for a, b in depth_pairs[i]
                for m, n in lat_pairs[j]
            ]
            corners.append(lax.ppermute(sent[4 + 2 * i + j], ("depth", "lat"), both))
    phase_next, heat_next, mine, outgoing = brick(
        ext, (*depth_halo, *lat_halo, *corners), iface_count
    )
    for bit, distance in enumerate((1, 2, 6, 8, 24, 56)):
        hops = [(i, i ^ distance) for i in range(depth_size)]
        theirs = lax.ppermute(outgoing, "depth", hops)
        if bit < 4:
            mine, outgoing = combine(bit, mine, theirs)
        elif bit == 4:
            mine = outgoing = combine_all(bit, mine, theirs)
        else:
            picture = last(bit, mine, theirs)
    return phase_next, heat_next, picture


def all_kernel(bit, mine, theirs, out):
    in_front = (lax.axis_index("depth") >> bit) & 1 == 0

    def write(c, value):
        out[:, c] = value

    @pl.when(in_front)
    def _():
        blend(mine, theirs, write)

    @pl.when(jnp.logical_not(in_front))
    def _():
        blend(theirs, mine, write)


def combine_all(bit, mine, theirs):
    return pl.pallas_call(
        functools.partial(all_kernel, bit),
        out_shape=jax.ShapeDtypeStruct(mine.shape, jnp.float32),
        in_specs=[VMEM] * 2,
        out_specs=VMEM,
        compiler_params=pltpu.CompilerParams(vmem_limit_bytes=8 << 20),
    )(mine, theirs)


def solution(mesh):
    return jax.shard_map(
        per_device,
        mesh=mesh,
        in_specs=(P("depth", "lat", None), P("depth", "lat", None), P("depth", "lat")),
        out_specs=(P("depth", "lat", None), P("depth", "lat", None), P(None, "lat", "depth")),
        check_vma=False,
    )
```

```python
import functools
import math

import jax
import jax.numpy as jnp
import numpy as np
from jax import lax
from jax.experimental import pallas as pl
from jax.experimental.pallas import tpu as pltpu
from jax.sharding import PartitionSpec as P

SWEEPS = 3
DIFFUSION = (0.5, 2.0)
TIME_STEP = 0.4
COUPLE = 0.6
LATENT = 0.5
SHEAR_Y = (1.6, -1.6, 0.8, -1.2)
SHEAR_Z = (0.9, -0.6, -0.9, 0.3)
CX, CY, NZ = 32, 64, 128
NX = 2048
VIEWS = 4

HALO = 3
RIM = 5
EX = CX + 2 * HALO
ROW0 = 8
EY = CY + 2 * ROW0
CORNER = 4
RELATIVE = (0, 3, 1, 2)


def thetas(sweep_total):
    chebyshev = []
    for f in range(2):
        highest = 1.0 + 12.0 * DIFFUSION[f]
        entries = [
            0.5 * (highest + 1.0)
            + 0.5 * (highest - 1.0) * math.cos((2 * j + 1) * math.pi / (2 * sweep_total))
            for j in range(sweep_total)
        ]
        chebyshev.append(entries)
    return np.array(chebyshev)


VMEM = pl.BlockSpec(memory_space=pltpu.VMEM)
SMEM = pl.BlockSpec(memory_space=pltpu.SMEM)
ANY = pl.BlockSpec(memory_space=pl.ANY)


HBM = pl.BlockSpec(memory_space=pltpu.HBM)
FIELD = jax.ShapeDtypeStruct((2, EX, EY, NZ), jnp.float32)
INNER = tuple(range(ROW0, ROW0 + CY, 8))
STRIPS = (ROW0 - CORNER, ROW0 + CY - CORNER)


def params(mib):
    return pltpu.CompilerParams(vmem_limit_bytes=mib << 20)


def odd(axis):
    return lax.rem(lax.axis_index(axis), 2)


def depth_pack(phase, temper):
    low = jnp.stack([phase[:HALO], temper[:HALO]])
    high = jnp.stack([phase[-HALO:], temper[-HALO:]])
    is_odd = odd("depth") == 1
    return jnp.where(is_odd, low, high), jnp.where(is_odd, high, low)


def lat_pack_kernel(ext, depth_a, depth_b, lat_a, lat_b):
    layer_a = (1 - odd("depth")) * (HALO + CX)
    layer_b = odd("depth") * (HALO + CX)
    row_a = (1 - odd("lat")) * (CY - RIM)
    row_b = odd("lat") * (CY - RIM)
    for f in range(2):
        for row, target in ((row_a, lat_a), (row_b, lat_b)):
            for x in range(CX):
                at = pl.ds((f * EX + HALO + x) * RIM, RIM)
                target[at, :] = ext[f, HALO + x, pl.ds(ROW0 + row, RIM), :]
            for k in range(HALO):
                for layer, halo in ((layer_a, depth_a), (layer_b, depth_b)):
                    at = pl.ds((f * EX + layer + k) * RIM, RIM)
                    target[at, :] = halo[f, k, pl.ds(row, RIM), :]


def lat_pack(ext, depth_a, depth_b):
    rows = jax.ShapeDtypeStruct((2 * EX * RIM, NZ), jnp.float32)
    return pl.pallas_call(
        lat_pack_kernel,
        out_shape=[rows, rows],
        in_specs=[VMEM] * 3,
        out_specs=[VMEM] * 2,
        compiler_params=params(4),
    )(ext, depth_a, depth_b)


def lat_unpack(ext, lat_a, lat_b):
    row_a = ROW0 - RIM + (1 - odd("lat")) * (RIM + CY)
    row_b = ROW0 - RIM + odd("lat") * (RIM + CY)
    for f in range(2):
        for x in range(EX):
            at = pl.ds((f * EX + x) * RIM, RIM)
            ext[f, x, pl.ds(row_a, RIM), :] = lat_a[at, :]
            ext[f, x, pl.ds(row_b, RIM), :] = lat_b[at, :]


def zero_layers(ref, first, last):
    depth = lax.axis_index("depth")

    @pl.when(depth == 0)
    def _():
        for f in range(2):
            for x in range(first, HALO):
                ref[f, x] = jnp.zeros((EY, NZ), jnp.float32)

    @pl.when(depth == lax.axis_size("depth") - 1)
    def _():
        for f in range(2):
            for x in range(HALO + CX, last):
                ref[f, x] = jnp.zeros((EY, NZ), jnp.float32)


def zero_rows(ref, first, last):
    lat = lax.axis_index("lat")

    def rows(row):
        def layer(x, carry):
            for f in range(2):
                ref[f, x, pl.ds(row, 8), :] = jnp.zeros((8, NZ), jnp.float32)
            return carry

        lax.fori_loop(first, last, layer, 0, unroll=2)

    @pl.when(lat == 0)
    def _():
        rows(0)

    @pl.when(lat == lax.axis_size("lat") - 1)
    def _():
        rows(ROW0 + CY)


def sweep(j, inp, out, source, first, last, rows, unroll):
    theta = thetas(SWEEPS)
    lane = lax.broadcasted_iota(jnp.int32, (8, NZ), 1)
    low_edge = lane == 0
    high_edge = lane == NZ - 1

    def layer(x, carry):
        for row in rows:
            centres = [inp[f, x, pl.ds(row, 8), :] for f in range(2)]
            if j == 0:
                p, h = centres
                reaction = TIME_STEP * (p * (1.0 - p) * ((p - 0.5) + COUPLE * h))
                sources = (
                    (p + reaction) * (1.0 / DIFFUSION[0]),
                    (h + LATENT * reaction) * (1.0 / DIFFUSION[1]),
                )
                for f in range(2):
                    source[f, x, pl.ds(row, 8), :] = sources[f]
            else:
                sources = [source[f, x, pl.ds(row, 8), :] for f in range(2)]
            for f in range(2):
                u = centres[f]
                around = inp[f, x - 1, pl.ds(row, 8), :] + inp[f, x + 1, pl.ds(row, 8), :]
                sides = inp[f, x, pl.ds(row - 1, 8), :] + inp[f, x, pl.ds(row + 1, 8), :]
                below = jnp.where(low_edge, 0.0, pltpu.roll(u, 1, 1))
                above = jnp.where(high_edge, 0.0, pltpu.roll(u, NZ - 1, 1))
                total = (around + sides) + ((below + above) + sources[f])
                k = DIFFUSION[f]
                inverse = 1.0 / theta[f, j]
                value = float(k * inverse) * total
                own = float(1.0 - (1.0 + 6.0 * k) * inverse)
                if 2 * j + 1 != SWEEPS:
                    value = value + own * u
                out[f, x, pl.ds(row, 8), :] = value
        return carry

    lax.fori_loop(first, last, layer, 0, unroll=unroll)


def first_kernel(phase, temper, ext, once, source):
    for f, field in enumerate((phase, temper)):

        def layer(x, carry):
            ext[f, HALO + x, pl.ds(ROW0, CY), :] = field[x]
            return carry

        lax.fori_loop(0, CX, layer, 0, unroll=4)
    sweep(0, ext, once, source, HALO + 1, HALO + CX - 1, INNER, 3)


def first(phase, temper):
    return pl.pallas_call(
        first_kernel,
        out_shape=[FIELD] * 3,
        in_specs=[VMEM] * 2,
        out_specs=[VMEM] * 3,
        compiler_params=params(4),
    )(phase, temper)


def inner_kernel(
    ext_in, once_in, source_in, depth_a, depth_b, lat_a, ext, once, source, twice, thrice
):
    del ext_in, once_in, source_in, lat_a
    layer_a = (1 - odd("depth")) * (HALO + CX)
    layer_b = odd("depth") * (HALO + CX)
    for f in range(2):
        for k in range(HALO):
            ext[f, layer_a + k, pl.ds(ROW0, CY), :] = depth_a[f, k]
            ext[f, layer_b + k, pl.ds(ROW0, CY), :] = depth_b[f, k]
    sweep(0, ext, once, source, 1, HALO + 1, INNER, 3)
    sweep(0, ext, once, source, HALO + CX - 1, EX - 1, INNER, 3)
    zero_layers(once, 1, EX - 1)
    sweep(1, once, twice, source, 2, EX - 2, INNER, 2)
    zero_layers(twice, 2, EX - 2)
    sweep(2, twice, thrice, source, HALO, HALO + CX, INNER, 4)


def inner(fields, halos, lat_a):
    return pl.pallas_call(
        inner_kernel,
        out_shape=[FIELD] * 5,
        in_specs=[VMEM] * 6,
        out_specs=[VMEM] * 5,
        input_output_aliases={0: 0, 1: 1, 2: 2},
        compiler_params=params(4),
    )(*fields, *halos, lat_a)


def whole_part(v, x):
    base = [math.floor(SHEAR_Y[v] * i / CX) for i in range(CX)]
    value = jnp.int32(base[0])
    for i in range(1, CX):
        if base[i] != base[i - 1]:
            value = value + jnp.where(x >= i, base[i] - base[i - 1], 0)
    return value


AT_ONCE = 2


def render(views, field, count, pic):
    lane = lax.broadcasted_iota(jnp.int32, (8, NZ), 1)
    scale = -4.0 / NX * math.log2(math.e)
    tiles = tuple(range(0, CY, 8))
    for v in views:
        for c in range(4):
            pic[v, c] = jnp.full((CY, NZ), 1.0 if c == 3 else 0.0, jnp.float32)

    def layers(i, carry):
        for v in views:
            positive = SHEAR_Z[v] > 0
            shift = NZ - 1 if positive else 1
            edge = (lane == NZ - 1) if positive else (lane == 0)
            places = []
            for q in range(AT_ONCE):
                x = i * AT_ONCE + q
                xf = x.astype(jnp.float32)
                base_y = whole_part(v, x)
                frac_y = xf * (SHEAR_Y[v] / CX) - base_y.astype(jnp.float32)
                frac_z = xf * (abs(SHEAR_Z[v]) / CX)
                far_z = jnp.where(edge, 0.0, frac_z)
                live = jnp.where(x < count, scale, 0.0)
                places.append((x, base_y, frac_y, 1.0 - frac_z, far_z, live))
            for t in tiles:
                at = pl.ds(t, 8)
                colours = [pic[v, c, at, :] for c in range(3)]
                trans = pic[v, 3, at, :]
                for x, base_y, frac_y, near_z, far_z, live in places:
                    samples = []
                    for f in range(2):
                        row = ROW0 + t + base_y
                        near = field[f, HALO + x, pl.ds(row, 8), :]
                        far = field[f, HALO + x, pl.ds(row + 1, 8), :]
                        mixed = near + frac_y * (far - near)
                        samples.append(mixed * near_z + pltpu.roll(mixed, shift, 1) * far_z)
                    s0, s1 = samples
                    passed = trans * jnp.exp2(s0 * s0 * live)
                    weight = trans - passed
                    trans = passed
                    square = s1 * s1
                    outer = square + 1.64
                    slope = 1.6 * s1
                    colours[0] = colours[0] + weight / (outer + slope)
                    colours[1] = colours[1] + weight / (square + 1.0)
                    colours[2] = colours[2] + weight / (outer - slope)
                for c in range(3):
                    pic[v, c, at, :] = colours[c]
                pic[v, 3, at, :] = trans
        return carry

    lax.fori_loop(0, lax.div(count + (AT_ONCE - 1), AT_ONCE), layers, 0)


def brick_kernel(
    ext_in, once_in, source_in, twice_in, thrice_in, lat_a, lat_b, count,
    phase_next, heat_next, keep, send, ext, once, source, twice, thrice,
    pic, turned, sems,
):
    del ext_in, once_in, source_in, twice_in, thrice_in
    lat_unpack(ext, lat_a, lat_b)
    sweep(0, ext, once, source, 1, EX - 1, STRIPS, 6)
    zero_layers(once, 1, EX - 1)
    zero_rows(once, 1, EX - 1)
    sweep(1, once, twice, source, 2, EX - 2, STRIPS, 2)
    zero_layers(twice, 2, EX - 2)
    zero_rows(twice, 2, EX - 2)
    sweep(2, twice, thrice, source, HALO, HALO + CX, STRIPS, 8)
    zero_rows(thrice, HALO, HALO + CX)
    copies = []
    for f, field in enumerate((phase_next, heat_next)):
        copies.append(
            pltpu.make_async_copy(
                thrice.at[f, pl.ds(HALO, CX), pl.ds(ROW0, CY), :], field, sems.at[f]
            )
        )
    for copy in copies:
        copy.start()
    render(range(VIEWS), thrice, count[0, 0], pic)
    for v in range(2):
        for c in range(4):
            square = jnp.concatenate([pic[v, c], pltpu.roll(pic[3 - v, c], 64, 1)], axis=0)
            turned[v, c] = square.T
    depth = lax.axis_index("depth")
    my_core = lax.rem(depth, 2)
    my_x = lax.rem(lax.div(depth, 2), 4)
    my_z = lax.div(depth, 8)
    my_class = jnp.where(my_z < 4, my_z, 7 - my_z)
    for core_rel, target in ((0, keep), (1, send)):
        for i, x_rel in enumerate(RELATIVE):
            for j, z_rel in enumerate(RELATIVE):
                group = my_class ^ z_rel
                block = (group & 1) * 8 + (my_x ^ x_rel) * 2 + (my_core ^ core_rel)
                for c in range(4):
                    target[i * 4 + j, c] = turned[
                        group >> 1, c, pl.ds(pl.multiple_of(block * 8, 8), 8), :
                    ]
    for copy in copies:
        copy.wait()


def brick(fields, lat_a, lat_b, iface_count):
    f32 = jnp.float32
    pieces = jax.ShapeDtypeStruct((16, 4, 8, NZ), f32)
    block = jax.ShapeDtypeStruct((CX, CY, NZ), f32)
    return pl.pallas_call(
        brick_kernel,
        out_shape=[block, block, pieces, pieces] + [FIELD] * 5,
        in_specs=[VMEM] * 7 + [SMEM],
        out_specs=[HBM, HBM] + [VMEM] * 7,
        input_output_aliases={i: 4 + i for i in range(5)},
        scratch_shapes=[
            pltpu.VMEM((VIEWS, 4, CY, NZ), f32),
            pltpu.VMEM((2, 4, NZ, 2 * CY), f32),
            pltpu.SemaphoreType.DMA((2,)),
        ],
        compiler_params=params(8),
    )(*fields, lat_a, lat_b, iface_count)[:4]


def blend(front, back, write):
    clear = front[:, 3]
    for c in range(3):
        write(c, front[:, c] + clear * back[:, c])
    write(3, clear * back[:, 3])


def combine_kernel(bit, mine, theirs, keep, send):
    half = keep.shape[0]
    in_front = (lax.axis_index("depth") >> bit) & 1 == 0

    def write(c, value):
        keep[:, c] = value[:half]
        send[:, c] = value[half:]

    @pl.when(in_front)
    def _():
        blend(mine, theirs, write)

    @pl.when(jnp.logical_not(in_front))
    def _():
        blend(theirs, mine, write)


def combine(bit, mine, theirs):
    half = jax.ShapeDtypeStruct((mine.shape[0] // 2,) + mine.shape[1:], jnp.float32)
    return pl.pallas_call(
        functools.partial(combine_kernel, bit),
        out_shape=[half, half],
        in_specs=[VMEM] * 2,
        out_specs=[VMEM] * 2,
        compiler_params=pltpu.CompilerParams(vmem_limit_bytes=4 << 20),
    )(mine, theirs)


def last_kernel(bit, mine, theirs, out, mixed):
    low_half = (lax.axis_index("depth") >> bit) & 1 == 0

    def write(c, value):
        mixed[pl.ds(c * 8, 8), :] = value[0]

    @pl.when(low_half)
    def _():
        blend(mine, theirs, write)

    @pl.when(jnp.logical_not(low_half))
    def _():
        blend(theirs, mine, write)

    value = mixed[...]
    value = jnp.where(low_half, value, pltpu.roll(value, 64, 1))
    for c in range(4):
        out[c] = value[c * 8 : c * 8 + 8, :CY]


def last(bit, mine, theirs):
    return pl.pallas_call(
        functools.partial(last_kernel, bit),
        out_shape=jax.ShapeDtypeStruct((4, 8, CY), jnp.float32),
        in_specs=[VMEM] * 2,
        out_specs=VMEM,
        scratch_shapes=[pltpu.VMEM((32, NZ), jnp.float32)],
        compiler_params=pltpu.CompilerParams(vmem_limit_bytes=4 << 20),
    )(mine, theirs).transpose(0, 2, 1)


def pairs(count, start):
    result = []
    for i in range(start, count - 1, 2):
        result += [(i, i + 1), (i + 1, i)]
    return result


def per_device(phase, temper, iface_count):
    depth_size = lax.axis_size("depth")
    lat_size = lax.axis_size("lat")
    depth_pairs = [pairs(depth_size, start) for start in range(2)]
    lat_pairs = [pairs(lat_size, start) for start in range(2)]
    halos = depth_pack(phase, temper)
    halos = [lax.ppermute(h, "depth", p) for h, p in zip(halos, depth_pairs)]
    fields = first(phase, temper)
    packed = lat_pack(fields[0], *halos)
    rims = [lax.ppermute(h, "lat", p) for h, p in zip(packed, lat_pairs)]
    fields = inner(fields, halos, packed[0])
    phase_next, heat_next, mine, outgoing = brick(fields, *rims, iface_count)
    for bit, distance in enumerate((1, 2, 6, 8, 24, 56)):
        hops = [(i, i ^ distance) for i in range(depth_size)]
        theirs = lax.ppermute(outgoing, "depth", hops)
        if bit < 4:
            mine, outgoing = combine(bit, mine, theirs)
        elif bit == 4:
            mine = outgoing = combine_all(bit, mine, theirs)
        else:
            picture = last(bit, mine, theirs)
    return phase_next, heat_next, picture


def all_kernel(bit, mine, theirs, out):
    in_front = (lax.axis_index("depth") >> bit) & 1 == 0

    def write(c, value):
        out[:, c] = value

    @pl.when(in_front)
    def _():
        blend(mine, theirs, write)

    @pl.when(jnp.logical_not(in_front))
    def _():
        blend(theirs, mine, write)


def combine_all(bit, mine, theirs):
    return pl.pallas_call(
        functools.partial(all_kernel, bit),
        out_shape=jax.ShapeDtypeStruct(mine.shape, jnp.float32),
        in_specs=[VMEM] * 2,
        out_specs=VMEM,
        compiler_params=pltpu.CompilerParams(vmem_limit_bytes=4 << 20),
    )(mine, theirs)


def solution(mesh):
    return jax.shard_map(
        per_device,
        mesh=mesh,
        in_specs=(P("depth", "lat", None), P("depth", "lat", None), P("depth", "lat")),
        out_specs=(P("depth", "lat", None), P("depth", "lat", None), P(None, "lat", "depth")),
        check_vma=False,
    )
```

```python
import functools
import math

import jax
import jax.numpy as jnp
import numpy as np
from jax import lax
from jax.experimental import pallas as pl
from jax.experimental.pallas import tpu as pltpu
from jax.sharding import PartitionSpec as P

SWEEPS = 3
DIFFUSION = (0.5, 2.0)
TIME_STEP = 0.4
COUPLE = 0.6
LATENT = 0.5
SHEAR_Y = (1.6, -1.6, 0.8, -1.2)
SHEAR_Z = (0.9, -0.6, -0.9, 0.3)
CX, CY, NZ = 32, 64, 128
NX = 2048
VIEWS = 4

HALO = 3
RIM = 5
EX = CX + 2 * HALO
ROW0 = 8
EY = CY + 2 * ROW0
CORNER = 4


def thetas(sweep_total):
    chebyshev = []
    for f in range(2):
        highest = 1.0 + 12.0 * DIFFUSION[f]
        entries = [
            0.5 * (highest + 1.0)
            + 0.5 * (highest - 1.0) * math.cos((2 * j + 1) * math.pi / (2 * sweep_total))
            for j in range(sweep_total)
        ]
        chebyshev.append(entries)
    return np.array(chebyshev)


VMEM = pl.BlockSpec(memory_space=pltpu.VMEM)
SMEM = pl.BlockSpec(memory_space=pltpu.SMEM)
ANY = pl.BlockSpec(memory_space=pl.ANY)


HBM = pl.BlockSpec(memory_space=pltpu.HBM)
FIELD = jax.ShapeDtypeStruct((2, EX, EY, NZ), jnp.float32)
INNER = tuple(range(ROW0, ROW0 + CY, 8))
STRIPS = (ROW0 - CORNER, ROW0 + CY - CORNER)


def params(mib):
    return pltpu.CompilerParams(vmem_limit_bytes=mib << 20)


def odd(axis):
    return lax.rem(lax.axis_index(axis), 2)


def depth_pack(fields):
    low = fields[:, :HALO]
    high = fields[:, -HALO:]
    is_odd = odd("depth") == 1
    return jnp.where(is_odd, low, high), jnp.where(is_odd, high, low)


def lat_pack_kernel(ext, depth_a, depth_b, lat_a, lat_b):
    layer_a = (1 - odd("depth")) * (HALO + CX)
    layer_b = odd("depth") * (HALO + CX)
    row_a = (1 - odd("lat")) * (CY - RIM)
    row_b = odd("lat") * (CY - RIM)
    for f in range(2):
        for row, target in ((row_a, lat_a), (row_b, lat_b)):
            for x in range(CX):
                at = pl.ds((f * EX + HALO + x) * RIM, RIM)
                target[at, :] = ext[f, HALO + x, pl.ds(ROW0 + row, RIM), :]
            for k in range(HALO):
                for layer, halo in ((layer_a, depth_a), (layer_b, depth_b)):
                    at = pl.ds((f * EX + layer + k) * RIM, RIM)
                    target[at, :] = halo[f, k, pl.ds(row, RIM), :]


def lat_pack(ext, depth_a, depth_b):
    rows = jax.ShapeDtypeStruct((2 * EX * RIM, NZ), jnp.float32)
    return pl.pallas_call(
        lat_pack_kernel,
        out_shape=[rows, rows],
        in_specs=[VMEM] * 3,
        out_specs=[VMEM] * 2,
        compiler_params=params(4),
    )(ext, depth_a, depth_b)


def lat_unpack(ext, lat_a, lat_b):
    row_a = ROW0 - RIM + (1 - odd("lat")) * (RIM + CY)
    row_b = ROW0 - RIM + odd("lat") * (RIM + CY)
    for f in range(2):
        for x in range(EX):
            at = pl.ds((f * EX + x) * RIM, RIM)
            ext[f, x, pl.ds(row_a, RIM), :] = lat_a[at, :]
            ext[f, x, pl.ds(row_b, RIM), :] = lat_b[at, :]


def zero_layers(ref, first, last):
    depth = lax.axis_index("depth")

    @pl.when(depth == 0)
    def _():
        for f in range(2):
            for x in range(first, HALO):
                ref[f, x] = jnp.zeros((EY, NZ), jnp.float32)

    @pl.when(depth == lax.axis_size("depth") - 1)
    def _():
        for f in range(2):
            for x in range(HALO + CX, last):
                ref[f, x] = jnp.zeros((EY, NZ), jnp.float32)


def zero_rows(ref, first, last):
    lat = lax.axis_index("lat")

    def rows(row):
        def layer(x, carry):
            for f in range(2):
                ref[f, x, pl.ds(row, 8), :] = jnp.zeros((8, NZ), jnp.float32)
            return carry

        lax.fori_loop(first, last, layer, 0, unroll=2)

    @pl.when(lat == 0)
    def _():
        rows(0)

    @pl.when(lat == lax.axis_size("lat") - 1)
    def _():
        rows(ROW0 + CY)


def sweep(j, inp, out, source, first, last, rows, unroll):
    theta = thetas(SWEEPS)
    lane = lax.broadcasted_iota(jnp.int32, (8, NZ), 1)
    low_edge = lane == 0
    high_edge = lane == NZ - 1

    def layer(x, carry):
        for row in rows:
            centres = [inp[f, x, pl.ds(row, 8), :] for f in range(2)]
            if j == 0:
                p, h = centres
                reaction = TIME_STEP * (p * (1.0 - p) * ((p - 0.5) + COUPLE * h))
                sources = (
                    (p + reaction) * (1.0 / DIFFUSION[0]),
                    (h + LATENT * reaction) * (1.0 / DIFFUSION[1]),
                )
                for f in range(2):
                    source[f, x, pl.ds(row, 8), :] = sources[f]
            else:
                sources = [source[f, x, pl.ds(row, 8), :] for f in range(2)]
            for f in range(2):
                u = centres[f]
                around = inp[f, x - 1, pl.ds(row, 8), :] + inp[f, x + 1, pl.ds(row, 8), :]
                sides = inp[f, x, pl.ds(row - 1, 8), :] + inp[f, x, pl.ds(row + 1, 8), :]
                below = jnp.where(low_edge, 0.0, pltpu.roll(u, 1, 1))
                above = jnp.where(high_edge, 0.0, pltpu.roll(u, NZ - 1, 1))
                total = (around + sides) + ((below + above) + sources[f])
                k = DIFFUSION[f]
                inverse = 1.0 / theta[f, j]
                value = float(k * inverse) * total
                own = float(1.0 - (1.0 + 6.0 * k) * inverse)
                if 2 * j + 1 != SWEEPS:
                    value = value + own * u
                out[f, x, pl.ds(row, 8), :] = value
        return carry

    lax.fori_loop(first, last, layer, 0, unroll=unroll)


def first_kernel(fields, ext, once, source):
    for f in range(2):

        def layer(x, carry):
            ext[f, HALO + x, pl.ds(ROW0, CY), :] = fields[f, x]
            return carry

        lax.fori_loop(0, CX, layer, 0, unroll=8)
    sweep(0, ext, once, source, HALO + 1, HALO + CX - 1, INNER, 5)


def first(fields):
    return pl.pallas_call(
        first_kernel,
        out_shape=[FIELD] * 3,
        in_specs=[VMEM],
        out_specs=[VMEM] * 3,
        compiler_params=params(4),
    )(fields)


def inner_kernel(
    ext_in, once_in, source_in, depth_a, depth_b, lat_a, ext, once, source, twice, thrice
):
    del ext_in, once_in, source_in, lat_a
    layer_a = (1 - odd("depth")) * (HALO + CX)
    layer_b = odd("depth") * (HALO + CX)
    for f in range(2):
        for k in range(HALO):
            ext[f, layer_a + k, pl.ds(ROW0, CY), :] = depth_a[f, k]
            ext[f, layer_b + k, pl.ds(ROW0, CY), :] = depth_b[f, k]
    sweep(0, ext, once, source, 1, HALO + 1, INNER, 3)
    sweep(0, ext, once, source, HALO + CX - 1, EX - 1, INNER, 3)
    zero_layers(once, 1, EX - 1)
    sweep(1, once, twice, source, 2, EX - 2, INNER, 17)
    zero_layers(twice, 2, EX - 2)
    sweep(2, twice, thrice, source, HALO, HALO + CX, INNER, 8)


def inner(fields, halos, lat_a):
    return pl.pallas_call(
        inner_kernel,
        out_shape=[FIELD] * 5,
        in_specs=[VMEM] * 6,
        out_specs=[VMEM] * 5,
        input_output_aliases={0: 0, 1: 1, 2: 2},
        compiler_params=params(4),
    )(*fields, *halos, lat_a)


def whole_part(v, x):
    base = [math.floor(SHEAR_Y[v] * i / CX) for i in range(CX)]
    value = jnp.int32(base[0])
    for i in range(1, CX):
        if base[i] != base[i - 1]:
            value = value + jnp.where(x >= i, base[i] - base[i - 1], 0)
    return value


AT_ONCE = 2


def render(views, field, count, pic):
    lane = lax.broadcasted_iota(jnp.int32, (8, NZ), 1)
    scale = -4.0 / NX * math.log2(math.e)
    tiles = tuple(range(0, CY, 8))
    for v in views:
        for c in range(4):
            pic[v, c] = jnp.full((CY, NZ), 1.0 if c == 3 else 0.0, jnp.float32)

    def layers(i, carry):
        for v in views:
            positive = SHEAR_Z[v] > 0
            shift = NZ - 1 if positive else 1
            edge = (lane == NZ - 1) if positive else (lane == 0)
            places = []
            for q in range(AT_ONCE):
                x = i * AT_ONCE + q
                xf = x.astype(jnp.float32)
                base_y = whole_part(v, x)
                frac_y = xf * (SHEAR_Y[v] / CX) - base_y.astype(jnp.float32)
                frac_z = xf * (abs(SHEAR_Z[v]) / CX)
                near_w = (1.0 - frac_y) * (1.0 - frac_z)
                far_w = frac_y * (1.0 - frac_z)
                side = jnp.where(edge, 0.0, jnp.full((8, NZ), frac_z) / (1.0 - frac_z))
                live = jnp.where(x < count, scale, 0.0)
                places.append((x, base_y, near_w, far_w, side, live))
            for t in tiles:
                at = pl.ds(t, 8)
                colours = [pic[v, c, at, :] for c in range(3)]
                trans = pic[v, 3, at, :]
                for x, base_y, near_w, far_w, side, live in places:
                    samples = []
                    for f in range(2):
                        row = ROW0 + t + base_y
                        near = field[f, HALO + x, pl.ds(row, 8), :]
                        far = field[f, HALO + x, pl.ds(row + 1, 8), :]
                        mixed = near * near_w + far * far_w
                        samples.append(mixed + pltpu.roll(mixed, shift, 1) * side)
                    s0, s1 = samples
                    passed = trans * jnp.exp2(s0 * s0 * live)
                    weight = trans - passed
                    trans = passed
                    square = s1 * s1
                    outer = square + 1.64
                    slope = 1.6 * s1
                    colours[0] = colours[0] + weight / (outer + slope)
                    colours[1] = colours[1] + weight / (square + 1.0)
                    colours[2] = colours[2] + weight / (outer - slope)
                for c in range(3):
                    pic[v, c, at, :] = colours[c]
                pic[v, 3, at, :] = trans
        return carry

    lax.fori_loop(0, lax.div(count + (AT_ONCE - 1), AT_ONCE), layers, 0)


def brick_kernel(
    ext_in, once_in, source_in, twice_in, thrice_in, lat_a, lat_b, count,
    phase_next, heat_next, keep, send, ext, once, source, twice, thrice,
    pic, turned, sems,
):
    del ext_in, once_in, source_in, twice_in, thrice_in
    lat_unpack(ext, lat_a, lat_b)
    sweep(0, ext, once, source, 1, EX - 1, STRIPS, 12)
    zero_layers(once, 1, EX - 1)
    zero_rows(once, 1, EX - 1)
    sweep(1, once, twice, source, 2, EX - 2, STRIPS, 17)
    zero_layers(twice, 2, EX - 2)
    zero_rows(twice, 2, EX - 2)
    sweep(2, twice, thrice, source, HALO, HALO + CX, STRIPS, 16)
    zero_rows(thrice, HALO, HALO + CX)
    copies = []
    for f, field in enumerate((phase_next, heat_next)):
        copies.append(
            pltpu.make_async_copy(
                thrice.at[f, pl.ds(HALO, CX), pl.ds(ROW0, CY), :], field, sems.at[f]
            )
        )
    for copy in copies:
        copy.start()
    render(range(VIEWS), thrice, count[0, 0], pic)
    for v in range(2):
        for c in range(4):
            square = jnp.concatenate([pic[v, c], pltpu.roll(pic[3 - v, c], 64, 1)], axis=0)
            turned[v, c] = square.T
    depth = lax.axis_index("depth")
    my_core = lax.rem(depth, 2)
    my_x = lax.rem(lax.div(depth, 2), 4)
    for core_rel, target in ((0, keep), (1, send)):
        for x_rel in range(4):
            block = (my_x ^ x_rel) * 2 + (my_core ^ core_rel)
            for z in range(4):
                at = pl.ds(pl.multiple_of((block + (z & 1) * 8) * 8, 8), 8)
                for c in range(4):
                    target[x_rel * 4 + z, c] = turned[z >> 1, c, at, :]
    for copy in copies:
        copy.wait()


def brick(fields, lat_a, lat_b, iface_count):
    f32 = jnp.float32
    pieces = jax.ShapeDtypeStruct((16, 4, 8, NZ), f32)
    block = jax.ShapeDtypeStruct((CX, CY, NZ), f32)
    return pl.pallas_call(
        brick_kernel,
        out_shape=[block, block, pieces, pieces] + [FIELD] * 5,
        in_specs=[VMEM] * 7 + [SMEM],
        out_specs=[HBM, HBM] + [VMEM] * 7,
        input_output_aliases={i: 4 + i for i in range(5)},
        scratch_shapes=[
            pltpu.VMEM((VIEWS, 4, CY, NZ), f32),
            pltpu.VMEM((2, 4, NZ, 2 * CY), f32),
            pltpu.SemaphoreType.DMA((2,)),
        ],
        compiler_params=params(8),
    )(*fields, lat_a, lat_b, iface_count)[:4]


def blend(front, back, write):
    clear = front[:, 3]
    for c in range(3):
        write(c, front[:, c] + clear * back[:, c])
    write(3, clear * back[:, 3])


def core_kernel(mine, theirs, *parts):
    in_front = lax.rem(lax.axis_index("depth"), 2) == 0

    def write(c, value):
        for i, part in enumerate(parts):
            part[:, c] = value[4 * i : 4 * i + 4]

    @pl.when(in_front)
    def _():
        blend(mine, theirs, write)

    @pl.when(jnp.logical_not(in_front))
    def _():
        blend(theirs, mine, write)


def core_combine(mine, theirs):
    part = jax.ShapeDtypeStruct((4,) + mine.shape[1:], jnp.float32)
    return pl.pallas_call(
        core_kernel,
        out_shape=[part] * 4,
        in_specs=[VMEM] * 2,
        out_specs=[VMEM] * 4,
        compiler_params=params(4),
    )(mine, theirs)


def x_kernel(*refs):
    parts, out = refs[:4], refs[4]
    my_x = lax.rem(lax.div(lax.axis_index("depth"), 2), 4)
    low = lax.broadcasted_iota(jnp.int32, (8, NZ), 1) < CY

    def ordered(place):
        for z in range(4):
            back = parts[3 ^ place]
            total = [back[z, c] for c in range(4)]
            for x in (2, 1, 0):
                front = parts[x ^ place]
                clear = front[z, 3]
                total = [front[z, c] + clear * total[c] for c in range(3)] + [clear * total[3]]
            for pair in range(2):
                a, b = total[2 * pair], total[2 * pair + 1]
                out[z, pair] = jnp.where(low, a, pltpu.roll(b, CY, 1))
                out[7 - z, pair] = jnp.where(low, pltpu.roll(a, CY, 1), b)

    for place in range(4):
        pl.when(my_x == place)(functools.partial(ordered, place))


def x_combine(parts):
    return pl.pallas_call(
        x_kernel,
        out_shape=jax.ShapeDtypeStruct((8, 2, 8, NZ), jnp.float32),
        in_specs=[VMEM] * 4,
        out_specs=VMEM,
        compiler_params=params(4),
    )(*parts)


def z_kernel(slabs, out):
    low = lax.broadcasted_iota(jnp.int32, (8, NZ), 1) < CY
    first_pair, second_pair = slabs[7, 0], slabs[7, 1]
    for z in range(6, -1, -1):
        ahead = slabs[z, 1]
        clear = jnp.where(low, pltpu.roll(ahead, CY, 1), ahead)
        first_pair = slabs[z, 0] + clear * first_pair
        second_pair = jnp.where(low, ahead, 0.0) + clear * second_pair
    out[0] = first_pair[:, :CY]
    out[1] = first_pair[:, CY:]
    out[2] = second_pair[:, :CY]
    out[3] = second_pair[:, CY:]


def z_combine(slabs):
    return pl.pallas_call(
        z_kernel,
        out_shape=jax.ShapeDtypeStruct((4, 8, CY), jnp.float32),
        in_specs=[VMEM],
        out_specs=VMEM,
        compiler_params=params(4),
    )(slabs).transpose(0, 2, 1)


def pairs(count, start):
    result = []
    for i in range(start, count - 1, 2):
        result += [(i, i + 1), (i + 1, i)]
    return result


def per_device(phase, temper, iface_count):
    depth_size = lax.axis_size("depth")
    lat_size = lax.axis_size("lat")
    depth_pairs = [pairs(depth_size, start) for start in range(2)]
    lat_pairs = [pairs(lat_size, start) for start in range(2)]
    fields = jnp.stack([phase, temper])
    halos = depth_pack(fields)
    halos = [lax.ppermute(h, "depth", p) for h, p in zip(halos, depth_pairs)]
    fields = first(fields)
    packed = lat_pack(fields[0], *halos)
    rims = [lax.ppermute(h, "lat", p) for h, p in zip(packed, lat_pairs)]
    fields = inner(fields, halos, packed[0])
    phase_next, heat_next, mine, outgoing = brick(fields, *rims, iface_count)

    def partner(value, distance):
        return lax.ppermute(value, "depth", [(i, i ^ distance) for i in range(depth_size)])

    parts = core_combine(mine, partner(outgoing, 1))
    parts = [parts[0]] + [partner(parts[k], 2 * k) for k in (1, 2, 3)]
    groups = [[z * 8 + i for z in range(depth_size // 8)] for i in range(8)]
    slabs = lax.all_to_all(
        x_combine(parts), "depth", 0, 0, tiled=True, axis_index_groups=groups
    )
    return phase_next, heat_next, z_combine(slabs)


def solution(mesh):
    return jax.shard_map(
        per_device,
        mesh=mesh,
        in_specs=(P("depth", "lat", None), P("depth", "lat", None), P("depth", "lat")),
        out_specs=(P("depth", "lat", None), P("depth", "lat", None), P(None, "lat", "depth")),
        check_vma=False,
    )
```

```python
import functools
import math

import jax
import jax.numpy as jnp
import numpy as np
from jax import lax
from jax.experimental import pallas as pl
from jax.experimental.pallas import tpu as pltpu
from jax.sharding import PartitionSpec as P

SWEEPS = 3
DIFFUSION = (0.5, 2.0)
TIME_STEP = 0.4
COUPLE = 0.6
LATENT = 0.5
SHEAR_Y = (1.6, -1.6, 0.8, -1.2)
SHEAR_Z = (0.9, -0.6, -0.9, 0.3)
CX, CY, NZ = 32, 64, 128
NX = 2048
VIEWS = 4

HALO = 3
RIM = 5
EX = CX + 2 * HALO
ROW0 = 8
EY = CY + 2 * ROW0
CORNER = 4


def thetas(sweep_total):
    chebyshev = []
    for f in range(2):
        highest = 1.0 + 12.0 * DIFFUSION[f]
        entries = [
            0.5 * (highest + 1.0)
            + 0.5 * (highest - 1.0) * math.cos((2 * j + 1) * math.pi / (2 * sweep_total))
            for j in range(sweep_total)
        ]
        chebyshev.append(entries)
    return np.array(chebyshev)


VMEM = pl.BlockSpec(memory_space=pltpu.VMEM)
SMEM = pl.BlockSpec(memory_space=pltpu.SMEM)
ANY = pl.BlockSpec(memory_space=pl.ANY)


HBM = pl.BlockSpec(memory_space=pltpu.HBM)
FIELD = jax.ShapeDtypeStruct((2, EX, EY, NZ), jnp.float32)
PICTURES = jax.ShapeDtypeStruct((VIEWS, 4, CY, NZ), jnp.float32)
INNER_TILES = tuple(range(8, CY - 8, 8))
OUTER_TILES = (0, CY - 8)
INNER = tuple(range(ROW0, ROW0 + CY, 8))
STRIPS = (ROW0 - CORNER, ROW0 + CY - CORNER)


def params(mib):
    return pltpu.CompilerParams(vmem_limit_bytes=mib << 20)


def odd(axis):
    return lax.rem(lax.axis_index(axis), 2)


def depth_pack(fields):
    low = fields[:, :HALO]
    high = fields[:, -HALO:]
    is_odd = odd("depth") == 1
    return jnp.where(is_odd, low, high), jnp.where(is_odd, high, low)


def lat_pack_kernel(ext, depth_a, depth_b, lat_a, lat_b):
    layer_a = (1 - odd("depth")) * (HALO + CX)
    layer_b = odd("depth") * (HALO + CX)
    row_a = (1 - odd("lat")) * (CY - RIM)
    row_b = odd("lat") * (CY - RIM)
    for f in range(2):
        for row, target in ((row_a, lat_a), (row_b, lat_b)):
            for x in range(CX):
                at = pl.ds((f * EX + HALO + x) * RIM, RIM)
                target[at, :] = ext[f, HALO + x, pl.ds(ROW0 + row, RIM), :]
            for k in range(HALO):
                for layer, halo in ((layer_a, depth_a), (layer_b, depth_b)):
                    at = pl.ds((f * EX + layer + k) * RIM, RIM)
                    target[at, :] = halo[f, k, pl.ds(row, RIM), :]


def lat_pack(ext, depth_a, depth_b):
    rows = jax.ShapeDtypeStruct((2 * EX * RIM, NZ), jnp.float32)
    return pl.pallas_call(
        lat_pack_kernel,
        out_shape=[rows, rows],
        in_specs=[VMEM] * 3,
        out_specs=[VMEM] * 2,
        compiler_params=params(4),
    )(ext, depth_a, depth_b)


def lat_unpack(ext, lat_a, lat_b):
    row_a = ROW0 - RIM + (1 - odd("lat")) * (RIM + CY)
    row_b = ROW0 - RIM + odd("lat") * (RIM + CY)
    for f in range(2):
        for x in range(EX):
            at = pl.ds((f * EX + x) * RIM, RIM)
            ext[f, x, pl.ds(row_a, RIM), :] = lat_a[at, :]
            ext[f, x, pl.ds(row_b, RIM), :] = lat_b[at, :]


def zero_layers(ref, first, last):
    depth = lax.axis_index("depth")

    @pl.when(depth == 0)
    def _():
        for f in range(2):
            for x in range(first, HALO):
                ref[f, x] = jnp.zeros((EY, NZ), jnp.float32)

    @pl.when(depth == lax.axis_size("depth") - 1)
    def _():
        for f in range(2):
            for x in range(HALO + CX, last):
                ref[f, x] = jnp.zeros((EY, NZ), jnp.float32)


def zero_rows(ref, first, last):
    lat = lax.axis_index("lat")

    def rows(row):
        def layer(x, carry):
            for f in range(2):
                ref[f, x, pl.ds(row, 8), :] = jnp.zeros((8, NZ), jnp.float32)
            return carry

        lax.fori_loop(first, last, layer, 0, unroll=2)

    @pl.when(lat == 0)
    def _():
        rows(0)

    @pl.when(lat == lax.axis_size("lat") - 1)
    def _():
        rows(ROW0 + CY)


def sweep(j, inp, out, source, first, last, rows, unroll):
    theta = thetas(SWEEPS)
    lane = lax.broadcasted_iota(jnp.int32, (8, NZ), 1)
    low_edge = lane == 0
    high_edge = lane == NZ - 1

    def layer(x, carry):
        for row in rows:
            centres = [inp[f, x, pl.ds(row, 8), :] for f in range(2)]
            if j == 0:
                p, h = centres
                reaction = TIME_STEP * (p * (1.0 - p) * ((p - 0.5) + COUPLE * h))
                sources = (
                    (p + reaction) * (1.0 / DIFFUSION[0]),
                    (h + LATENT * reaction) * (1.0 / DIFFUSION[1]),
                )
                for f in range(2):
                    source[f, x, pl.ds(row, 8), :] = sources[f]
            else:
                sources = [source[f, x, pl.ds(row, 8), :] for f in range(2)]
            for f in range(2):
                u = centres[f]
                around = inp[f, x - 1, pl.ds(row, 8), :] + inp[f, x + 1, pl.ds(row, 8), :]
                sides = inp[f, x, pl.ds(row - 1, 8), :] + inp[f, x, pl.ds(row + 1, 8), :]
                below = jnp.where(low_edge, 0.0, pltpu.roll(u, 1, 1))
                above = jnp.where(high_edge, 0.0, pltpu.roll(u, NZ - 1, 1))
                total = (around + sides) + ((below + above) + sources[f])
                k = DIFFUSION[f]
                inverse = 1.0 / theta[f, j]
                value = float(k * inverse) * total
                own = float(1.0 - (1.0 + 6.0 * k) * inverse)
                if 2 * j + 1 != SWEEPS:
                    value = value + own * u
                out[f, x, pl.ds(row, 8), :] = value
        return carry

    lax.fori_loop(first, last, layer, 0, unroll=unroll)


def first_kernel(fields, ext, once, source, twice, thrice):
    for f in range(2):

        def layer(x, carry):
            ext[f, HALO + x, pl.ds(ROW0, CY), :] = fields[f, x]
            return carry

        lax.fori_loop(0, CX, layer, 0, unroll=8)
    sweep(0, ext, once, source, HALO + 1, HALO + CX - 1, INNER, 5)
    sweep(1, once, twice, source, HALO + 2, HALO + CX - 2, INNER, 14)
    sweep(2, twice, thrice, source, HALO + 3, HALO + CX - 3, INNER, 13)


def first(fields):
    return pl.pallas_call(
        first_kernel,
        out_shape=[FIELD] * 5,
        in_specs=[VMEM],
        out_specs=[VMEM] * 5,
        compiler_params=params(4),
    )(fields)


def inner_kernel(*refs):
    depth_a, depth_b, unused_lat, count = refs[5:9]
    ext, once, source, twice, thrice, pic = refs[9:]
    layer_a = (1 - odd("depth")) * (HALO + CX)
    layer_b = odd("depth") * (HALO + CX)
    for f in range(2):
        for k in range(HALO):
            ext[f, layer_a + k, pl.ds(ROW0, CY), :] = depth_a[f, k]
            ext[f, layer_b + k, pl.ds(ROW0, CY), :] = depth_b[f, k]
    for j, (inp, out) in enumerate(((ext, once), (once, twice), (twice, thrice))):
        for start in (1 + j, HALO + CX - 1 - j):
            sweep(j, inp, out, source, start, start + 3, INNER, 3)
        if j < 2:
            zero_layers(out, 1 + j, EX - 1 - j)
    render(INNER_TILES, 2, thrice, count[0, 0], pic)


def inner(fields, halos, lat_a, iface_count):
    return pl.pallas_call(
        inner_kernel,
        out_shape=[FIELD] * 5 + [PICTURES],
        in_specs=[VMEM] * 8 + [SMEM],
        out_specs=[VMEM] * 6,
        input_output_aliases={i: i for i in range(5)},
        compiler_params=params(4),
        cost_estimate=pl.CostEstimate(
            flops=40_000_000, bytes_accessed=1 << 20, transcendentals=0
        ),
    )(*fields, *halos, lat_a, iface_count)


def whole_part(v, x):
    base = [math.floor(SHEAR_Y[v] * i / CX) for i in range(CX)]
    value = jnp.int32(base[0])
    for i in range(1, CX):
        if base[i] != base[i - 1]:
            value = value + jnp.where(x >= i, base[i] - base[i - 1], 0)
    return value


def render(tiles, at_once, field, count, pic):
    lane = lax.broadcasted_iota(jnp.int32, (8, NZ), 1)
    scale = -4.0 / NX * math.log2(math.e)
    for v in range(VIEWS):
        for c in range(4):
            for t in tiles:
                pic[v, c, pl.ds(t, 8), :] = jnp.full((8, NZ), 1.0 if c == 3 else 0.0)

    def layers(i, carry):
        for v in range(VIEWS):
            positive = SHEAR_Z[v] > 0
            shift = NZ - 1 if positive else 1
            edge = (lane == NZ - 1) if positive else (lane == 0)
            places = []
            for q in range(at_once):
                x = i * at_once + q
                xf = x.astype(jnp.float32)
                base_y = whole_part(v, x)
                frac_y = xf * (SHEAR_Y[v] / CX) - base_y.astype(jnp.float32)
                frac_z = xf * (abs(SHEAR_Z[v]) / CX)
                near_w = (1.0 - frac_y) * (1.0 - frac_z)
                far_w = frac_y * (1.0 - frac_z)
                side = jnp.where(edge, 0.0, jnp.full((8, NZ), frac_z) / (1.0 - frac_z))
                live = jnp.where(x < count, scale, 0.0)
                places.append((x, base_y, near_w, far_w, side, live))
            for t in tiles:
                at = pl.ds(t, 8)
                colours = [pic[v, c, at, :] for c in range(3)]
                trans = pic[v, 3, at, :]
                for x, base_y, near_w, far_w, side, live in places:
                    samples = []
                    for f in range(2):
                        row = ROW0 + t + base_y
                        near = field[f, HALO + x, pl.ds(row, 8), :]
                        far = field[f, HALO + x, pl.ds(row + 1, 8), :]
                        mixed = near * near_w + far * far_w
                        samples.append(mixed + pltpu.roll(mixed, shift, 1) * side)
                    s0, s1 = samples
                    passed = trans * jnp.exp2(s0 * s0 * live)
                    weight = trans - passed
                    trans = passed
                    square = s1 * s1
                    outer = square + 1.64
                    slope = 1.6 * s1
                    colours[0] = colours[0] + weight / (outer + slope)
                    colours[1] = colours[1] + weight / (square + 1.0)
                    colours[2] = colours[2] + weight / (outer - slope)
                for c in range(3):
                    pic[v, c, at, :] = colours[c]
                pic[v, 3, at, :] = trans
        return carry

    lax.fori_loop(0, lax.div(count + (at_once - 1), at_once), layers, 0)


def brick_kernel(*refs):
    lat_a, lat_b, count = refs[6:9]
    keep, send, ext, once, source, twice, thrice, pic, turned = refs[9:]
    lat_unpack(ext, lat_a, lat_b)
    sweep(0, ext, once, source, 1, EX - 1, STRIPS, 12)
    zero_layers(once, 1, EX - 1)
    zero_rows(once, 1, EX - 1)
    sweep(1, once, twice, source, 2, EX - 2, STRIPS, 17)
    zero_layers(twice, 2, EX - 2)
    zero_rows(twice, 2, EX - 2)
    sweep(2, twice, thrice, source, HALO, HALO + CX, STRIPS, 16)
    zero_rows(thrice, HALO, HALO + CX)
    render(OUTER_TILES, 4, thrice, count[0, 0], pic)
    for v in range(2):
        for c in range(4):
            square = jnp.concatenate([pic[v, c], pltpu.roll(pic[3 - v, c], 64, 1)], axis=0)
            turned[v, c] = square.T
    depth = lax.axis_index("depth")
    my_core = lax.rem(depth, 2)
    my_x = lax.rem(lax.div(depth, 2), 4)
    for core_rel, target in ((0, keep), (1, send)):
        for x_rel in range(4):
            block = (my_x ^ x_rel) * 2 + (my_core ^ core_rel)
            for z in range(4):
                at = pl.ds(pl.multiple_of((block + (z & 1) * 8) * 8, 8), 8)
                for c in range(4):
                    target[x_rel * 4 + z, c] = turned[z >> 1, c, at, :]


def brick(fields, lat_a, lat_b, iface_count):
    pieces = jax.ShapeDtypeStruct((16, 4, 8, NZ), jnp.float32)
    results = pl.pallas_call(
        brick_kernel,
        out_shape=[pieces, pieces] + [FIELD] * 5 + [PICTURES],
        in_specs=[VMEM] * 8 + [SMEM],
        out_specs=[VMEM] * 8,
        input_output_aliases={i: 2 + i for i in range(6)},
        scratch_shapes=[pltpu.VMEM((2, 4, NZ, 2 * CY), jnp.float32)],
        compiler_params=params(4),
    )(*fields, lat_a, lat_b, iface_count)
    return results[0], results[1], results[6]


def emit_kernel(field, part, phase_next, heat_next, token, sems):
    copies = []
    for f, target in enumerate((phase_next, heat_next)):
        copies.append(
            pltpu.make_async_copy(
                field.at[f, pl.ds(HALO, CX), pl.ds(ROW0, CY), :], target, sems.at[f]
            )
        )
        copies[f].start()
    token[...] = part[0, 0]
    for copy in copies:
        copy.wait()


def emit(field, part):
    block = jax.ShapeDtypeStruct((CX, CY, NZ), jnp.float32)
    return pl.pallas_call(
        emit_kernel,
        out_shape=[block, block, jax.ShapeDtypeStruct((8, NZ), jnp.float32)],
        in_specs=[VMEM, VMEM],
        out_specs=[HBM, HBM, VMEM],
        scratch_shapes=[pltpu.SemaphoreType.DMA((2,))],
        compiler_params=params(4),
    )(field, part)


def blend(front, back, write):
    clear = front[:, 3]
    for c in range(3):
        write(c, front[:, c] + clear * back[:, c])
    write(3, clear * back[:, 3])


def core_kernel(mine, theirs, *parts):
    in_front = lax.rem(lax.axis_index("depth"), 2) == 0

    def write(c, value):
        for i, part in enumerate(parts):
            part[:, c] = value[4 * i : 4 * i + 4]

    @pl.when(in_front)
    def _():
        blend(mine, theirs, write)

    @pl.when(jnp.logical_not(in_front))
    def _():
        blend(theirs, mine, write)


def core_combine(mine, theirs):
    part = jax.ShapeDtypeStruct((4,) + mine.shape[1:], jnp.float32)
    return pl.pallas_call(
        core_kernel,
        out_shape=[part] * 4,
        in_specs=[VMEM] * 2,
        out_specs=[VMEM] * 4,
        compiler_params=params(4),
    )(mine, theirs)


def x_kernel(*refs):
    parts, out = refs[:4], refs[5]
    my_x = lax.rem(lax.div(lax.axis_index("depth"), 2), 4)
    low = lax.broadcasted_iota(jnp.int32, (8, NZ), 1) < CY

    def ordered(place):
        for z in range(4):
            back = parts[3 ^ place]
            total = [back[z, c] for c in range(4)]
            for x in (2, 1, 0):
                front = parts[x ^ place]
                clear = front[z, 3]
                total = [front[z, c] + clear * total[c] for c in range(3)] + [clear * total[3]]
            for pair in range(2):
                a, b = total[2 * pair], total[2 * pair + 1]
                out[z, pair] = jnp.where(low, a, pltpu.roll(b, CY, 1))
                out[7 - z, pair] = jnp.where(low, pltpu.roll(a, CY, 1), b)

    for place in range(4):
        pl.when(my_x == place)(functools.partial(ordered, place))


def x_combine(parts, token):
    return pl.pallas_call(
        x_kernel,
        out_shape=jax.ShapeDtypeStruct((8, 2, 8, NZ), jnp.float32),
        in_specs=[VMEM] * 5,
        out_specs=VMEM,
        compiler_params=params(4),
    )(*parts, token)


def z_kernel(slabs, out):
    low = lax.broadcasted_iota(jnp.int32, (8, NZ), 1) < CY
    first_pair, second_pair = slabs[7, 0], slabs[7, 1]
    for z in range(6, -1, -1):
        ahead = slabs[z, 1]
        clear = jnp.where(low, pltpu.roll(ahead, CY, 1), ahead)
        first_pair = slabs[z, 0] + clear * first_pair
        second_pair = jnp.where(low, ahead, 0.0) + clear * second_pair
    out[0] = first_pair[:, :CY]
    out[1] = first_pair[:, CY:]
    out[2] = second_pair[:, :CY]
    out[3] = second_pair[:, CY:]


def z_combine(slabs):
    return pl.pallas_call(
        z_kernel,
        out_shape=jax.ShapeDtypeStruct((4, 8, CY), jnp.float32),
        in_specs=[VMEM],
        out_specs=VMEM,
        compiler_params=params(4),
    )(slabs).transpose(0, 2, 1)


def pairs(count, start):
    result = []
    for i in range(start, count - 1, 2):
        result += [(i, i + 1), (i + 1, i)]
    return result


def per_device(phase, temper, iface_count):
    depth_size = lax.axis_size("depth")
    lat_size = lax.axis_size("lat")
    depth_pairs = [pairs(depth_size, start) for start in range(2)]
    lat_pairs = [pairs(lat_size, start) for start in range(2)]
    fields = jnp.stack([phase, temper])
    halos = depth_pack(fields)
    halos = [lax.ppermute(h, "depth", p) for h, p in zip(halos, depth_pairs)]
    fields = first(fields)
    packed = lat_pack(fields[0], *halos)
    rims = [lax.ppermute(h, "lat", p) for h, p in zip(packed, lat_pairs)]
    fields = inner(fields, halos, packed[0], iface_count)
    mine, outgoing, solved = brick(fields, *rims, iface_count)

    def partner(value, distance):
        return lax.ppermute(value, "depth", [(i, i ^ distance) for i in range(depth_size)])

    parts = core_combine(mine, partner(outgoing, 1))
    phase_next, heat_next, token = emit(solved, parts[0])
    parts = [parts[0]] + [partner(parts[k], 2 * k) for k in (1, 2, 3)]
    groups = [[z * 8 + i for z in range(depth_size // 8)] for i in range(8)]
    slabs = lax.all_to_all(
        x_combine(parts, token), "depth", 0, 0, tiled=True, axis_index_groups=groups
    )
    return phase_next, heat_next, z_combine(slabs)


def solution(mesh):
    return jax.shard_map(
        per_device,
        mesh=mesh,
        in_specs=(P("depth", "lat", None), P("depth", "lat", None), P("depth", "lat")),
        out_specs=(P("depth", "lat", None), P("depth", "lat", None), P(None, "lat", "depth")),
        check_vma=False,
    )
```

```python
import functools
import math

import jax
import jax.numpy as jnp
import numpy as np
from jax import lax
from jax.experimental import pallas as pl
from jax.experimental.pallas import tpu as pltpu
from jax.sharding import PartitionSpec as P

SWEEPS = 3
DIFFUSION = (0.5, 2.0)
TIME_STEP = 0.4
COUPLE = 0.6
LATENT = 0.5
SHEAR_Y = (1.6, -1.6, 0.8, -1.2)
SHEAR_Z = (0.9, -0.6, -0.9, 0.3)
CX, CY, NZ = 32, 64, 128
NX = 2048
VIEWS = 4

HALO = 3
RIM = 5
EX = CX + 2 * HALO
ROW0 = 8
EY = CY + 2 * ROW0
CORNER = 4


def thetas(sweep_total):
    chebyshev = []
    for f in range(2):
        highest = 1.0 + 12.0 * DIFFUSION[f]
        entries = [
            0.5 * (highest + 1.0)
            + 0.5 * (highest - 1.0) * math.cos((2 * j + 1) * math.pi / (2 * sweep_total))
            for j in range(sweep_total)
        ]
        chebyshev.append(entries)
    return np.array(chebyshev)


VMEM = pl.BlockSpec(memory_space=pltpu.VMEM)
SMEM = pl.BlockSpec(memory_space=pltpu.SMEM)
ANY = pl.BlockSpec(memory_space=pl.ANY)


HBM = pl.BlockSpec(memory_space=pltpu.HBM)
FIELD = jax.ShapeDtypeStruct((2, EX, EY, NZ), jnp.float32)
PICTURES = jax.ShapeDtypeStruct((VIEWS, 4, CY, NZ), jnp.float32)
INNER_TILES = tuple(range(8, CY - 8, 8))
OUTER_TILES = (0, CY - 8)
INNER = tuple(range(ROW0, ROW0 + CY, 8))
STRIPS = (ROW0 - CORNER, ROW0 + CY - CORNER)


def params(mib):
    return pltpu.CompilerParams(vmem_limit_bytes=mib << 20)


def odd(axis):
    return lax.rem(lax.axis_index(axis), 2)


def depth_pack(fields):
    low = fields[:, :HALO]
    high = fields[:, -HALO:]
    is_odd = odd("depth") == 1
    return jnp.where(is_odd, low, high), jnp.where(is_odd, high, low)


def lat_pack_kernel(ext, depth_a, depth_b, lat_a, lat_b):
    layer_a = (1 - odd("depth")) * (HALO + CX)
    layer_b = odd("depth") * (HALO + CX)
    row_a = (1 - odd("lat")) * (CY - RIM)
    row_b = odd("lat") * (CY - RIM)
    for f in range(2):
        for row, target in ((row_a, lat_a), (row_b, lat_b)):
            for x in range(CX):
                at = pl.ds((f * EX + HALO + x) * RIM, RIM)
                target[at, :] = ext[f, HALO + x, pl.ds(ROW0 + row, RIM), :]
            for k in range(HALO):
                for layer, halo in ((layer_a, depth_a), (layer_b, depth_b)):
                    at = pl.ds((f * EX + layer + k) * RIM, RIM)
                    target[at, :] = halo[f, k, pl.ds(row, RIM), :]


def lat_pack(ext, depth_a, depth_b):
    rows = jax.ShapeDtypeStruct((2 * EX * RIM, NZ), jnp.float32)
    return pl.pallas_call(
        lat_pack_kernel,
        out_shape=[rows, rows],
        in_specs=[VMEM] * 3,
        out_specs=[VMEM] * 2,
        compiler_params=params(4),
    )(ext, depth_a, depth_b)


def lat_unpack(ext, lat_a, lat_b):
    row_a = ROW0 - RIM + (1 - odd("lat")) * (RIM + CY)
    row_b = ROW0 - RIM + odd("lat") * (RIM + CY)
    for f in range(2):
        for x in range(EX):
            at = pl.ds((f * EX + x) * RIM, RIM)
            ext[f, x, pl.ds(row_a, RIM), :] = lat_a[at, :]
            ext[f, x, pl.ds(row_b, RIM), :] = lat_b[at, :]


def zero_layers(ref, first, last):
    depth = lax.axis_index("depth")

    @pl.when(depth == 0)
    def _():
        for f in range(2):
            for x in range(first, HALO):
                ref[f, x] = jnp.zeros((EY, NZ), jnp.float32)

    @pl.when(depth == lax.axis_size("depth") - 1)
    def _():
        for f in range(2):
            for x in range(HALO + CX, last):
                ref[f, x] = jnp.zeros((EY, NZ), jnp.float32)


def zero_rows(ref, first, last):
    lat = lax.axis_index("lat")

    def rows(row):
        def layer(x, carry):
            for f in range(2):
                ref[f, x, pl.ds(row, 8), :] = jnp.zeros((8, NZ), jnp.float32)
            return carry

        lax.fori_loop(first, last, layer, 0, unroll=2)

    @pl.when(lat == 0)
    def _():
        rows(0)

    @pl.when(lat == lax.axis_size("lat") - 1)
    def _():
        rows(ROW0 + CY)


def sweep(j, inp, out, source, first, last, rows, unroll):
    theta = thetas(SWEEPS)
    lane = lax.broadcasted_iota(jnp.int32, (8, NZ), 1)
    low_edge = lane == 0
    high_edge = lane == NZ - 1

    def layer(x, carry):
        for row in rows:
            centres = [inp[f, x, pl.ds(row, 8), :] for f in range(2)]
            if j == 0:
                p, h = centres
                reaction = TIME_STEP * (p * (1.0 - p) * ((p - 0.5) + COUPLE * h))
                sources = (
                    (p + reaction) * (1.0 / DIFFUSION[0]),
                    (h + LATENT * reaction) * (1.0 / DIFFUSION[1]),
                )
                for f in range(2):
                    source[f, x, pl.ds(row, 8), :] = sources[f]
            else:
                sources = [source[f, x, pl.ds(row, 8), :] for f in range(2)]
            for f in range(2):
                u = centres[f]
                around = inp[f, x - 1, pl.ds(row, 8), :] + inp[f, x + 1, pl.ds(row, 8), :]
                sides = inp[f, x, pl.ds(row - 1, 8), :] + inp[f, x, pl.ds(row + 1, 8), :]
                below = jnp.where(low_edge, 0.0, pltpu.roll(u, 1, 1))
                above = jnp.where(high_edge, 0.0, pltpu.roll(u, NZ - 1, 1))
                total = (around + sides) + ((below + above) + sources[f])
                k = DIFFUSION[f]
                inverse = 1.0 / theta[f, j]
                value = float(k * inverse) * total
                own = float(1.0 - (1.0 + 6.0 * k) * inverse)
                if 2 * j + 1 != SWEEPS:
                    value = value + own * u
                out[f, x, pl.ds(row, 8), :] = value
        return carry

    lax.fori_loop(first, last, layer, 0, unroll=unroll)


def first_kernel(fields, ext, once, source, twice):
    for f in range(2):

        def layer(x, carry):
            ext[f, HALO + x, pl.ds(ROW0, CY), :] = fields[f, x]
            return carry

        lax.fori_loop(0, CX, layer, 0, unroll=8)
    sweep(0, ext, once, source, HALO + 1, HALO + CX - 1, INNER, 5)
    sweep(1, once, twice, source, HALO + 2, HALO + CX - 2, INNER, 14)


def first(fields):
    return pl.pallas_call(
        first_kernel,
        out_shape=[FIELD] * 4,
        in_specs=[VMEM],
        out_specs=[VMEM] * 4,
        compiler_params=params(4),
    )(fields)


def inner_kernel(*refs):
    depth_a, depth_b, unused_lat, count = refs[4:8]
    ext, once, source, twice, thrice, pic = refs[8:]
    layer_a = (1 - odd("depth")) * (HALO + CX)
    layer_b = odd("depth") * (HALO + CX)
    for f in range(2):
        for k in range(HALO):
            ext[f, layer_a + k, pl.ds(ROW0, CY), :] = depth_a[f, k]
            ext[f, layer_b + k, pl.ds(ROW0, CY), :] = depth_b[f, k]
    zero_layers(ext, 0, EX)
    for j, (inp, out) in enumerate(((ext, once), (once, twice))):
        for start in (1 + j, HALO + CX - 1 - j):
            sweep(j, inp, out, source, start, start + 3, INNER, 3)
        zero_layers(out, 1 + j, EX - 1 - j)
    sweep(2, twice, thrice, source, HALO, HALO + CX, INNER, 16)
    render(INNER_TILES, 4, thrice, count[0, 0], pic)


def inner(fields, halos, lat_a, iface_count):
    return pl.pallas_call(
        inner_kernel,
        out_shape=[FIELD] * 5 + [PICTURES],
        in_specs=[VMEM] * 7 + [SMEM],
        out_specs=[VMEM] * 6,
        input_output_aliases={i: i for i in range(4)},
        compiler_params=params(4),
        cost_estimate=pl.CostEstimate(
            flops=40_000_000, bytes_accessed=1 << 20, transcendentals=0
        ),
    )(*fields, *halos, lat_a, iface_count)


CENTRE = 0.8
SHRINK = 0.5 / CENTRE


def whole_part(v, x):
    base = [math.floor(SHEAR_Y[v] * i / CX) for i in range(CX)]
    value = jnp.int32(base[0])
    for i in range(1, CX):
        if base[i] != base[i - 1]:
            value = value + jnp.where(x >= i, base[i] - base[i - 1], 0)
    return value


def render(tiles, at_once, field, count, pic):
    lane = lax.broadcasted_iota(jnp.int32, (8, NZ), 1)
    scale = -4.0 / NX * math.log2(math.e)
    for v in range(VIEWS):
        for c in range(4):
            for t in tiles:
                pic[v, c, pl.ds(t, 8), :] = jnp.full((8, NZ), 1.0 if c == 3 else 0.0)

    def layers(i, carry):
        for v in range(VIEWS):
            positive = SHEAR_Z[v] > 0
            shift = NZ - 1 if positive else 1
            edge = (lane == NZ - 1) if positive else (lane == 0)
            places = []
            for q in range(at_once):
                x = i * at_once + q
                xf = x.astype(jnp.float32)
                base_y = whole_part(v, x)
                frac_y = xf * (SHEAR_Y[v] / CX) - base_y.astype(jnp.float32)
                frac_z = xf * (abs(SHEAR_Z[v]) / CX)
                own = (1.0 - frac_y) * (1.0 - frac_z)
                ratio = jnp.full((8, NZ), frac_y) / (1.0 - frac_y)
                side = jnp.where(edge, 0.0, jnp.full((8, NZ), frac_z) / (1.0 - frac_z))
                live = jnp.where(x < count, scale * own * own, 0.0)
                places.append((x, base_y, ratio, side, live, own * SHRINK))
            for t in tiles:
                at = pl.ds(t, 8)
                colours = [pic[v, c, at, :] for c in range(3)]
                trans = pic[v, 3, at, :]
                for x, base_y, ratio, side, live, own in places:
                    samples = []
                    for f in range(2):
                        row = ROW0 + t + base_y
                        near = field[f, HALO + x, pl.ds(row, 8), :]
                        far = field[f, HALO + x, pl.ds(row + 1, 8), :]
                        mixed = near + far * ratio
                        samples.append(mixed + pltpu.roll(mixed, shift, 1) * side)
                    passed = trans * jnp.exp2(samples[0] * samples[0] * live)
                    weight = trans - passed
                    trans = passed
                    p = samples[1] * own
                    square = p * p
                    outer = square + (1.0 + CENTRE * CENTRE) * SHRINK * SHRINK
                    colours[0] = colours[0] + weight / (outer + p)
                    colours[1] = colours[1] + weight / (square + SHRINK * SHRINK)
                    colours[2] = colours[2] + weight / (outer - p)
                for c in range(3):
                    pic[v, c, at, :] = colours[c]
                pic[v, 3, at, :] = trans
        return carry

    lax.fori_loop(0, lax.div(count + (at_once - 1), at_once), layers, 0)


def brick_kernel(*refs):
    lat_a, lat_b, count = refs[6:9]
    keep, send, ext, once, source, twice, thrice, pic, turned = refs[9:]
    lat_unpack(ext, lat_a, lat_b)
    zero_layers(ext, 0, EX)
    zero_rows(ext, 0, EX)
    sweep(0, ext, once, source, 1, EX - 1, STRIPS, 12)
    zero_layers(once, 1, EX - 1)
    zero_rows(once, 1, EX - 1)
    sweep(1, once, twice, source, 2, EX - 2, STRIPS, 17)
    zero_layers(twice, 2, EX - 2)
    zero_rows(twice, 2, EX - 2)
    sweep(2, twice, thrice, source, HALO, HALO + CX, STRIPS, 16)
    zero_rows(thrice, HALO, HALO + CX)
    render(OUTER_TILES, 4, thrice, count[0, 0], pic)
    for v in range(2):
        for c in range(4):
            square = jnp.concatenate([pic[v, c], pltpu.roll(pic[3 - v, c], 64, 1)], axis=0)
            if c < 3:
                square = square * (SHRINK * SHRINK)
            turned[v, c] = square.T
    depth = lax.axis_index("depth")
    my_core = lax.rem(depth, 2)
    my_x = lax.rem(lax.div(depth, 2), 4)
    for core_rel, target in ((0, keep), (1, send)):
        for x_rel in range(4):
            block = (my_x ^ x_rel) * 2 + (my_core ^ core_rel)
            for z in range(4):
                at = pl.ds(pl.multiple_of((block + (z & 1) * 8) * 8, 8), 8)
                for c in range(4):
                    target[x_rel * 4 + z, c] = turned[z >> 1, c, at, :]


def brick(fields, lat_a, lat_b, iface_count):
    pieces = jax.ShapeDtypeStruct((16, 4, 8, NZ), jnp.float32)
    results = pl.pallas_call(
        brick_kernel,
        out_shape=[pieces, pieces] + [FIELD] * 5 + [PICTURES],
        in_specs=[VMEM] * 8 + [SMEM],
        out_specs=[VMEM] * 8,
        input_output_aliases={i: 2 + i for i in range(6)},
        scratch_shapes=[pltpu.VMEM((2, 4, NZ, 2 * CY), jnp.float32)],
        compiler_params=params(4),
    )(*fields, lat_a, lat_b, iface_count)
    return results[0], results[1], results[6]


def emit_kernel(field, part, phase_next, heat_next, token, sems):
    copies = []
    for f, target in enumerate((phase_next, heat_next)):
        copies.append(
            pltpu.make_async_copy(
                field.at[f, pl.ds(HALO, CX), pl.ds(ROW0, CY), :], target, sems.at[f]
            )
        )
        copies[f].start()
    token[...] = part[0, 0]
    for copy in copies:
        copy.wait()


def emit(field, part):
    block = jax.ShapeDtypeStruct((CX, CY, NZ), jnp.float32)
    return pl.pallas_call(
        emit_kernel,
        out_shape=[block, block, jax.ShapeDtypeStruct((8, NZ), jnp.float32)],
        in_specs=[VMEM, VMEM],
        out_specs=[HBM, HBM, VMEM],
        scratch_shapes=[pltpu.SemaphoreType.DMA((2,))],
        compiler_params=params(4),
    )(field, part)


def blend(front, back, write):
    clear = front[:, 3]
    for c in range(3):
        write(c, front[:, c] + clear * back[:, c])
    write(3, clear * back[:, 3])


def core_kernel(mine, theirs, *parts):
    in_front = lax.rem(lax.axis_index("depth"), 2) == 0

    def write(c, value):
        for i, part in enumerate(parts):
            part[:, c] = value[4 * i : 4 * i + 4]

    @pl.when(in_front)
    def _():
        blend(mine, theirs, write)

    @pl.when(jnp.logical_not(in_front))
    def _():
        blend(theirs, mine, write)


def core_combine(mine, theirs):
    part = jax.ShapeDtypeStruct((4,) + mine.shape[1:], jnp.float32)
    return pl.pallas_call(
        core_kernel,
        out_shape=[part] * 4,
        in_specs=[VMEM] * 2,
        out_specs=[VMEM] * 4,
        compiler_params=params(4),
    )(mine, theirs)


def x_kernel(*refs):
    parts, out = refs[:4], refs[5]
    my_x = lax.rem(lax.div(lax.axis_index("depth"), 2), 4)
    low = lax.broadcasted_iota(jnp.int32, (8, NZ), 1) < CY

    def ordered(place):
        for z in range(4):
            back = parts[3 ^ place]
            total = [back[z, c] for c in range(4)]
            for x in (2, 1, 0):
                front = parts[x ^ place]
                clear = front[z, 3]
                total = [front[z, c] + clear * total[c] for c in range(3)] + [clear * total[3]]
            for pair in range(2):
                a, b = total[2 * pair], total[2 * pair + 1]
                out[z, pair] = jnp.where(low, a, pltpu.roll(b, CY, 1))
                out[7 - z, pair] = jnp.where(low, pltpu.roll(a, CY, 1), b)

    for place in range(4):
        pl.when(my_x == place)(functools.partial(ordered, place))


def x_combine(parts, token):
    return pl.pallas_call(
        x_kernel,
        out_shape=jax.ShapeDtypeStruct((8, 2, 8, NZ), jnp.float32),
        in_specs=[VMEM] * 5,
        out_specs=VMEM,
        compiler_params=params(4),
    )(*parts, token)


def z_kernel(slabs, out):
    low = lax.broadcasted_iota(jnp.int32, (8, NZ), 1) < CY
    first_pair, second_pair = slabs[7, 0], slabs[7, 1]
    for z in range(6, -1, -1):
        ahead = slabs[z, 1]
        clear = jnp.where(low, pltpu.roll(ahead, CY, 1), ahead)
        first_pair = slabs[z, 0] + clear * first_pair
        second_pair = jnp.where(low, ahead, 0.0) + clear * second_pair
    out[0] = first_pair[:, :CY]
    out[1] = first_pair[:, CY:]
    out[2] = second_pair[:, :CY]
    out[3] = second_pair[:, CY:]


def z_combine(slabs):
    return pl.pallas_call(
        z_kernel,
        out_shape=jax.ShapeDtypeStruct((4, 8, CY), jnp.float32),
        in_specs=[VMEM],
        out_specs=VMEM,
        compiler_params=params(4),
    )(slabs).transpose(0, 2, 1)


RING_D = 1
RING_L = 1


def pairs(count, start, ring):
    result = []
    for i in range(start, count if ring else count - 1, 2):
        after = (i + 1) % count
        result += [(i, after), (after, i)]
    return result


def per_device(phase, temper, iface_count):
    depth_size = lax.axis_size("depth")
    lat_size = lax.axis_size("lat")
    depth_pairs = [pairs(depth_size, start, RING_D) for start in range(2)]
    lat_pairs = [pairs(lat_size, start, RING_L) for start in range(2)]
    fields = jnp.stack([phase, temper])
    halos = depth_pack(fields)
    halos = [lax.ppermute(h, "depth", p) for h, p in zip(halos, depth_pairs)]
    fields = first(fields)
    packed = lat_pack(fields[0], *halos)
    rims = [lax.ppermute(h, "lat", p) for h, p in zip(packed, lat_pairs)]
    fields = inner(fields, halos, packed[0], iface_count)
    mine, outgoing, solved = brick(fields, *rims, iface_count)

    def partner(value, distance):
        return lax.ppermute(value, "depth", [(i, i ^ distance) for i in range(depth_size)])

    parts = core_combine(mine, partner(outgoing, 1))
    phase_next, heat_next, token = emit(solved, parts[0])
    parts = [parts[0]] + [partner(parts[k], 2 * k) for k in (1, 2, 3)]
    groups = [[z * 8 + i for z in range(depth_size // 8)] for i in range(8)]
    slabs = lax.all_to_all(
        x_combine(parts, token), "depth", 0, 0, tiled=True, axis_index_groups=groups
    )
    return phase_next, heat_next, z_combine(slabs)


def solution(mesh):
    return jax.shard_map(
        per_device,
        mesh=mesh,
        in_specs=(P("depth", "lat", None), P("depth", "lat", None), P("depth", "lat")),
        out_specs=(P("depth", "lat", None), P("depth", "lat", None), P(None, "lat", "depth")),
        check_vma=False,
    )
```

```python
import functools
import math

import jax
import jax.numpy as jnp
import numpy as np
from jax import lax
from jax.experimental import pallas as pl
from jax.experimental.pallas import tpu as pltpu
from jax.sharding import PartitionSpec as P

SWEEPS = 3
DIFFUSION = (0.5, 2.0)
TIME_STEP = 0.4
COUPLE = 0.6
LATENT = 0.5
SHEAR_Y = (1.6, -1.6, 0.8, -1.2)
SHEAR_Z = (0.9, -0.6, -0.9, 0.3)
CX, CY, NZ = 32, 64, 128
NX = 2048
VIEWS = 4

HALO = 3
RIM = 5
EX = CX + 2 * HALO
ROW0 = 8
EY = CY + 2 * ROW0
CORNER = 4


def thetas(sweep_total):
    chebyshev = []
    for f in range(2):
        highest = 1.0 + 12.0 * DIFFUSION[f]
        entries = [
            0.5 * (highest + 1.0)
            + 0.5 * (highest - 1.0) * math.cos((2 * j + 1) * math.pi / (2 * sweep_total))
            for j in range(sweep_total)
        ]
        chebyshev.append(entries)
    return np.array(chebyshev)


VMEM = pl.BlockSpec(memory_space=pltpu.VMEM)
SMEM = pl.BlockSpec(memory_space=pltpu.SMEM)
ANY = pl.BlockSpec(memory_space=pl.ANY)


HBM = pl.BlockSpec(memory_space=pltpu.HBM)
FIELD = jax.ShapeDtypeStruct((2, EX, EY, NZ), jnp.float32)
PICTURES = jax.ShapeDtypeStruct((VIEWS, 4, CY, NZ), jnp.float32)
INNER_TILES = tuple(range(8, CY - 8, 8))
OUTER_TILES = (0, CY - 8)
INNER = tuple(range(ROW0, ROW0 + CY, 8))
STRIPS = (ROW0 - CORNER, ROW0 + CY - CORNER)


def params(mib):
    return pltpu.CompilerParams(vmem_limit_bytes=mib << 20)


def odd(axis):
    return lax.rem(lax.axis_index(axis), 2)


def depth_pack(fields):
    low = fields[:, :HALO]
    high = fields[:, -HALO:]
    is_odd = odd("depth") == 1
    return jnp.where(is_odd, low, high), jnp.where(is_odd, high, low)


def lat_pack_kernel(ext, depth_a, depth_b, lat_a, lat_b):
    layer_a = (1 - odd("depth")) * (HALO + CX)
    layer_b = odd("depth") * (HALO + CX)
    row_a = (1 - odd("lat")) * (CY - RIM)
    row_b = odd("lat") * (CY - RIM)
    for f in range(2):
        for row, target in ((row_a, lat_a), (row_b, lat_b)):
            for x in range(CX):
                at = pl.ds((f * EX + HALO + x) * RIM, RIM)
                target[at, :] = ext[f, HALO + x, pl.ds(ROW0 + row, RIM), :]
            for k in range(HALO):
                for layer, halo in ((layer_a, depth_a), (layer_b, depth_b)):
                    at = pl.ds((f * EX + layer + k) * RIM, RIM)
                    target[at, :] = halo[f, k, pl.ds(row, RIM), :]


def lat_pack(ext, depth_a, depth_b):
    rows = jax.ShapeDtypeStruct((2 * EX * RIM, NZ), jnp.float32)
    return pl.pallas_call(
        lat_pack_kernel,
        out_shape=[rows, rows],
        in_specs=[VMEM] * 3,
        out_specs=[VMEM] * 2,
        compiler_params=params(4),
    )(ext, depth_a, depth_b)


def lat_unpack(ext, lat_a, lat_b):
    row_a = ROW0 - RIM + (1 - odd("lat")) * (RIM + CY)
    row_b = ROW0 - RIM + odd("lat") * (RIM + CY)
    for f in range(2):
        for x in range(EX):
            at = pl.ds((f * EX + x) * RIM, RIM)
            ext[f, x, pl.ds(row_a, RIM), :] = lat_a[at, :]
            ext[f, x, pl.ds(row_b, RIM), :] = lat_b[at, :]


def zero_layers(ref, first, last):
    depth = lax.axis_index("depth")

    @pl.when(depth == 0)
    def _():
        for f in range(2):
            for x in range(first, HALO):
                ref[f, x] = jnp.zeros((EY, NZ), jnp.float32)

    @pl.when(depth == lax.axis_size("depth") - 1)
    def _():
        for f in range(2):
            for x in range(HALO + CX, last):
                ref[f, x] = jnp.zeros((EY, NZ), jnp.float32)


def zero_rows(ref, first, last):
    lat = lax.axis_index("lat")

    def rows(row):
        def layer(x, carry):
            for f in range(2):
                ref[f, x, pl.ds(row, 8), :] = jnp.zeros((8, NZ), jnp.float32)
            return carry

        lax.fori_loop(first, last, layer, 0, unroll=2)

    @pl.when(lat == 0)
    def _():
        rows(0)

    @pl.when(lat == lax.axis_size("lat") - 1)
    def _():
        rows(ROW0 + CY)


def sweep(j, inp, out, source, first, last, rows, unroll):
    theta = thetas(SWEEPS)
    lane = lax.broadcasted_iota(jnp.int32, (8, NZ), 1)
    low_edge = lane == 0
    high_edge = lane == NZ - 1

    def layer(x, carry):
        for row in rows:
            centres = [inp[f, x, pl.ds(row, 8), :] for f in range(2)]
            if j == 0:
                p, h = centres
                reaction = TIME_STEP * (p * (1.0 - p) * ((p - 0.5) + COUPLE * h))
                sources = (
                    (p + reaction) * (1.0 / DIFFUSION[0]),
                    (h + LATENT * reaction) * (1.0 / DIFFUSION[1]),
                )
                for f in range(2):
                    source[f, x, pl.ds(row, 8), :] = sources[f]
            else:
                sources = [source[f, x, pl.ds(row, 8), :] for f in range(2)]
            for f in range(2):
                u = centres[f]
                around = inp[f, x - 1, pl.ds(row, 8), :] + inp[f, x + 1, pl.ds(row, 8), :]
                sides = inp[f, x, pl.ds(row - 1, 8), :] + inp[f, x, pl.ds(row + 1, 8), :]
                below = jnp.where(low_edge, 0.0, pltpu.roll(u, 1, 1))
                above = jnp.where(high_edge, 0.0, pltpu.roll(u, NZ - 1, 1))
                total = (around + sides) + ((below + above) + sources[f])
                k = DIFFUSION[f]
                inverse = 1.0 / theta[f, j]
                value = float(k * inverse) * total
                own = float(1.0 - (1.0 + 6.0 * k) * inverse)
                if 2 * j + 1 != SWEEPS:
                    value = value + own * u
                out[f, x, pl.ds(row, 8), :] = value
        return carry

    lax.fori_loop(first, last, layer, 0, unroll=unroll)


def first_kernel(fields, ext, once, source, twice, thrice):
    for f in range(2):

        def layer(x, carry):
            ext[f, HALO + x, pl.ds(ROW0, CY), :] = fields[f, x]
            return carry

        lax.fori_loop(0, CX, layer, 0, unroll=8)
    sweep(0, ext, once, source, HALO + 1, HALO + CX - 1, INNER, 5)
    sweep(1, once, twice, source, HALO + 2, HALO + CX - 2, INNER, 14)
    sweep(2, twice, thrice, source, HALO + 3, HALO + CX - 3, INNER, 13)


def first(fields):
    return pl.pallas_call(
        first_kernel,
        out_shape=[FIELD] * 5,
        in_specs=[VMEM],
        out_specs=[VMEM] * 5,
        compiler_params=params(4),
    )(fields)


def inner_kernel(*refs):
    depth_a, depth_b, unused_lat, count = refs[5:9]
    ext, once, source, twice, thrice, pic = refs[9:]
    layer_a = (1 - odd("depth")) * (HALO + CX)
    layer_b = odd("depth") * (HALO + CX)
    for f in range(2):
        for k in range(HALO):
            ext[f, layer_a + k, pl.ds(ROW0, CY), :] = depth_a[f, k]
            ext[f, layer_b + k, pl.ds(ROW0, CY), :] = depth_b[f, k]
    zero_layers(ext, 0, EX)
    for j, (inp, out) in enumerate(((ext, once), (once, twice), (twice, thrice))):
        for start in (1 + j, HALO + CX - 1 - j):
            sweep(j, inp, out, source, start, start + 3, INNER, 3)
        if j < 2:
            zero_layers(out, 1 + j, EX - 1 - j)
    render(INNER_TILES, 4, thrice, count[0, 0], pic)


def inner(fields, halos, lat_a, iface_count):
    return pl.pallas_call(
        inner_kernel,
        out_shape=[FIELD] * 5 + [PICTURES],
        in_specs=[VMEM] * 8 + [SMEM],
        out_specs=[VMEM] * 6,
        input_output_aliases={i: i for i in range(5)},
        compiler_params=params(4),
        cost_estimate=pl.CostEstimate(
            flops=40_000_000, bytes_accessed=1 << 20, transcendentals=0
        ),
    )(*fields, *halos, lat_a, iface_count)


CENTRE = 0.8
SHRINK = 0.5 / CENTRE


def whole_part(v, x):
    base = [math.floor(SHEAR_Y[v] * i / CX) for i in range(CX)]
    value = jnp.int32(base[0])
    for i in range(1, CX):
        if base[i] != base[i - 1]:
            value = value + jnp.where(x >= i, base[i] - base[i - 1], 0)
    return value


def render(tiles, at_once, field, count, pic):
    lane = lax.broadcasted_iota(jnp.int32, (8, NZ), 1)
    scale = -4.0 / NX * math.log2(math.e)
    for v in range(VIEWS):
        for c in range(4):
            for t in tiles:
                pic[v, c, pl.ds(t, 8), :] = jnp.full((8, NZ), 1.0 if c == 3 else 0.0)

    def layers(i, carry):
        for v in range(VIEWS):
            positive = SHEAR_Z[v] > 0
            shift = NZ - 1 if positive else 1
            edge = (lane == NZ - 1) if positive else (lane == 0)
            places = []
            for q in range(at_once):
                x = i * at_once + q
                xf = x.astype(jnp.float32)
                base_y = whole_part(v, x)
                frac_y = xf * (SHEAR_Y[v] / CX) - base_y.astype(jnp.float32)
                frac_z = xf * (abs(SHEAR_Z[v]) / CX)
                own = (1.0 - frac_y) * (1.0 - frac_z)
                ratio = jnp.full((8, NZ), frac_y) / (1.0 - frac_y)
                side = jnp.where(edge, 0.0, jnp.full((8, NZ), frac_z) / (1.0 - frac_z))
                live = jnp.where(x < count, scale * own * own, 0.0)
                places.append((x, base_y, ratio, side, live, own * SHRINK))
            for t in tiles:
                at = pl.ds(t, 8)
                colours = [pic[v, c, at, :] for c in range(3)]
                trans = pic[v, 3, at, :]
                for x, base_y, ratio, side, live, own in places:
                    samples = []
                    for f in range(2):
                        row = ROW0 + t + base_y
                        near = field[f, HALO + x, pl.ds(row, 8), :]
                        far = field[f, HALO + x, pl.ds(row + 1, 8), :]
                        mixed = near + far * ratio
                        samples.append(mixed + pltpu.roll(mixed, shift, 1) * side)
                    passed = trans * jnp.exp2(samples[0] * samples[0] * live)
                    weight = trans - passed
                    trans = passed
                    p = samples[1] * own
                    square = p * p
                    outer = square + (1.0 + CENTRE * CENTRE) * SHRINK * SHRINK
                    colours[0] = colours[0] + weight / (outer + p)
                    colours[1] = colours[1] + weight / (square + SHRINK * SHRINK)
                    colours[2] = colours[2] + weight / (outer - p)
                for c in range(3):
                    pic[v, c, at, :] = colours[c]
                pic[v, 3, at, :] = trans
        return carry

    lax.fori_loop(0, lax.div(count + (at_once - 1), at_once), layers, 0)


def brick_kernel(*refs):
    lat_a, lat_b, count = refs[6:9]
    keep, send, ext, once, source, twice, thrice, pic, turned = refs[9:]
    lat_unpack(ext, lat_a, lat_b)
    zero_layers(ext, 0, EX)
    zero_rows(ext, 0, EX)
    sweep(0, ext, once, source, 1, EX - 1, STRIPS, 12)
    zero_layers(once, 1, EX - 1)
    zero_rows(once, 1, EX - 1)
    sweep(1, once, twice, source, 2, EX - 2, STRIPS, 17)
    zero_layers(twice, 2, EX - 2)
    zero_rows(twice, 2, EX - 2)
    sweep(2, twice, thrice, source, HALO, HALO + CX, STRIPS, 16)
    zero_rows(thrice, HALO, HALO + CX)
    render(OUTER_TILES, 8, thrice, count[0, 0], pic)
    for v in range(2):
        for c in range(4):
            square = jnp.concatenate([pic[v, c], pltpu.roll(pic[3 - v, c], 64, 1)], axis=0)
            if c < 3:
                square = square * (SHRINK * SHRINK)
            turned[v, c] = square.T
    depth = lax.axis_index("depth")
    my_core = lax.rem(depth, 2)
    my_x = lax.rem(lax.div(depth, 2), 4)
    for core_rel, target in ((0, keep), (1, send)):
        for x_rel in range(4):
            block = (my_x ^ x_rel) * 2 + (my_core ^ core_rel)
            for z in range(4):
                at = pl.ds(pl.multiple_of((block + (z & 1) * 8) * 8, 8), 8)
                for c in range(4):
                    target[x_rel * 4 + z, c] = turned[z >> 1, c, at, :]


def brick(fields, lat_a, lat_b, iface_count):
    pieces = jax.ShapeDtypeStruct((16, 4, 8, NZ), jnp.float32)
    results = pl.pallas_call(
        brick_kernel,
        out_shape=[pieces, pieces] + [FIELD] * 5 + [PICTURES],
        in_specs=[VMEM] * 8 + [SMEM],
        out_specs=[VMEM] * 8,
        input_output_aliases={i: 2 + i for i in range(6)},
        scratch_shapes=[pltpu.VMEM((2, 4, NZ, 2 * CY), jnp.float32)],
        compiler_params=params(4),
    )(*fields, lat_a, lat_b, iface_count)
    return results[0], results[1], results[6]


def emit_kernel(field, part, phase_next, heat_next, token, sems):
    copies = []
    for f, target in enumerate((phase_next, heat_next)):
        copies.append(
            pltpu.make_async_copy(
                field.at[f, pl.ds(HALO, CX), pl.ds(ROW0, CY), :], target, sems.at[f]
            )
        )
        copies[f].start()
    token[...] = part[0, 0]
    for copy in copies:
        copy.wait()


def emit(field, part):
    block = jax.ShapeDtypeStruct((CX, CY, NZ), jnp.float32)
    return pl.pallas_call(
        emit_kernel,
        out_shape=[block, block, jax.ShapeDtypeStruct((8, NZ), jnp.float32)],
        in_specs=[VMEM, VMEM],
        out_specs=[HBM, HBM, VMEM],
        scratch_shapes=[pltpu.SemaphoreType.DMA((2,))],
        compiler_params=params(4),
    )(field, part)


def blend(front, back, write):
    clear = front[:, 3]
    for c in range(3):
        write(c, front[:, c] + clear * back[:, c])
    write(3, clear * back[:, 3])


def core_kernel(mine, theirs, token, *parts):
    del token
    in_front = lax.rem(lax.axis_index("depth"), 2) == 0

    def write(c, value):
        for i, part in enumerate(parts):
            part[:, c] = value[4 * i : 4 * i + 4]

    @pl.when(in_front)
    def _():
        blend(mine, theirs, write)

    @pl.when(jnp.logical_not(in_front))
    def _():
        blend(theirs, mine, write)


def core_combine(mine, theirs, token):
    part = jax.ShapeDtypeStruct((4,) + mine.shape[1:], jnp.float32)
    return pl.pallas_call(
        core_kernel,
        out_shape=[part] * 4,
        in_specs=[VMEM] * 3,
        out_specs=[VMEM] * 4,
        compiler_params=params(4),
    )(mine, theirs, token)


def x_kernel(*refs):
    parts, out = refs[:4], refs[4]
    my_x = lax.rem(lax.div(lax.axis_index("depth"), 2), 4)
    low = lax.broadcasted_iota(jnp.int32, (8, NZ), 1) < CY

    def ordered(place):
        for z in range(4):
            back = parts[3 ^ place]
            total = [back[z, c] for c in range(4)]
            for x in (2, 1, 0):
                front = parts[x ^ place]
                clear = front[z, 3]
                total = [front[z, c] + clear * total[c] for c in range(3)] + [clear * total[3]]
            for pair in range(2):
                a, b = total[2 * pair], total[2 * pair + 1]
                out[z, pair] = jnp.where(low, a, pltpu.roll(b, CY, 1))
                out[7 - z, pair] = jnp.where(low, pltpu.roll(a, CY, 1), b)

    for place in range(4):
        pl.when(my_x == place)(functools.partial(ordered, place))


def x_combine(parts):
    return pl.pallas_call(
        x_kernel,
        out_shape=jax.ShapeDtypeStruct((8, 2, 8, NZ), jnp.float32),
        in_specs=[VMEM] * 4,
        out_specs=VMEM,
        compiler_params=params(4),
    )(*parts)


def z_kernel(slabs, out):
    low = lax.broadcasted_iota(jnp.int32, (8, NZ), 1) < CY
    first_pair, second_pair = slabs[7, 0], slabs[7, 1]
    for z in range(6, -1, -1):
        ahead = slabs[z, 1]
        clear = jnp.where(low, pltpu.roll(ahead, CY, 1), ahead)
        first_pair = slabs[z, 0] + clear * first_pair
        second_pair = jnp.where(low, ahead, 0.0) + clear * second_pair
    out[0] = first_pair[:, :CY]
    out[1] = first_pair[:, CY:]
    out[2] = second_pair[:, :CY]
    out[3] = second_pair[:, CY:]


def z_combine(slabs):
    return pl.pallas_call(
        z_kernel,
        out_shape=jax.ShapeDtypeStruct((4, 8, CY), jnp.float32),
        in_specs=[VMEM],
        out_specs=VMEM,
        compiler_params=params(4),
    )(slabs).transpose(0, 2, 1)


def pairs(count, start):
    result = []
    for i in range(start, count, 2):
        after = (i + 1) % count
        result += [(i, after), (after, i)]
    return result


def per_device(phase, temper, iface_count):
    depth_size = lax.axis_size("depth")
    lat_size = lax.axis_size("lat")
    depth_pairs = [pairs(depth_size, start) for start in range(2)]
    lat_pairs = [pairs(lat_size, start) for start in range(2)]
    fields = jnp.stack([phase, temper])
    halos = depth_pack(fields)
    halos = [lax.ppermute(h, "depth", p) for h, p in zip(halos, depth_pairs)]
    fields = first(fields)
    packed = lat_pack(fields[0], *halos)
    rims = [lax.ppermute(h, "lat", p) for h, p in zip(packed, lat_pairs)]
    fields = inner(fields, halos, packed[0], iface_count)
    mine, outgoing, solved = brick(fields, *rims, iface_count)

    def partner(value, distance):
        return lax.ppermute(value, "depth", [(i, i ^ distance) for i in range(depth_size)])

    theirs = partner(outgoing, 1)
    phase_next, heat_next, token = emit(solved, mine)
    parts = core_combine(mine, theirs, token)
    parts = [parts[0]] + [partner(parts[k], 2 * k) for k in (1, 2, 3)]
    groups = [[z * 8 + i for z in range(depth_size // 8)] for i in range(8)]
    slabs = lax.all_to_all(
        x_combine(parts), "depth", 0, 0, tiled=True, axis_index_groups=groups
    )
    return phase_next, heat_next, z_combine(slabs)


def solution(mesh):
    return jax.shard_map(
        per_device,
        mesh=mesh,
        in_specs=(P("depth", "lat", None), P("depth", "lat", None), P("depth", "lat")),
        out_specs=(P("depth", "lat", None), P("depth", "lat", None), P(None, "lat", "depth")),
        check_vma=False,
    )
```

```python
import functools
import math

import jax
import jax.numpy as jnp
import numpy as np
from jax import lax
from jax.experimental import pallas as pl
from jax.experimental.pallas import tpu as pltpu
from jax.sharding import PartitionSpec as P

SWEEPS = 3
DIFFUSION = (0.5, 2.0)
TIME_STEP = 0.4
COUPLE = 0.6
LATENT = 0.5
SHEAR_Y = (1.6, -1.6, 0.8, -1.2)
SHEAR_Z = (0.9, -0.6, -0.9, 0.3)
CX, CY, NZ = 32, 64, 128
NX = 2048
VIEWS = 4

HALO = 3
RIM = 5
EX = CX + 2 * HALO
ROW0 = 8
EY = CY + 2 * ROW0
CORNER = 4


def thetas(sweep_total):
    chebyshev = []
    for f in range(2):
        highest = 1.0 + 12.0 * DIFFUSION[f]
        entries = [
            0.5 * (highest + 1.0)
            + 0.5 * (highest - 1.0) * math.cos((2 * j + 1) * math.pi / (2 * sweep_total))
            for j in range(sweep_total)
        ]
        chebyshev.append(entries)
    return np.array(chebyshev)


VMEM = pl.BlockSpec(memory_space=pltpu.VMEM)
SMEM = pl.BlockSpec(memory_space=pltpu.SMEM)
ANY = pl.BlockSpec(memory_space=pl.ANY)


HBM = pl.BlockSpec(memory_space=pltpu.HBM)
FIELD = jax.ShapeDtypeStruct((2, EX, EY, NZ), jnp.float32)
PICTURES = jax.ShapeDtypeStruct((VIEWS, 4, CY, NZ), jnp.float32)
INNER_TILES = tuple(range(8, CY - 8, 8))
OUTER_TILES = (0, CY - 8)
INNER = tuple(range(ROW0, ROW0 + CY, 8))
STRIPS = (ROW0 - CORNER, ROW0 + CY - CORNER)


def params(mib):
    return pltpu.CompilerParams(vmem_limit_bytes=mib << 20)


def odd(axis):
    return lax.rem(lax.axis_index(axis), 2)


def depth_pack(fields):
    low = fields[:, :HALO]
    high = fields[:, -HALO:]
    is_odd = odd("depth") == 1
    return jnp.where(is_odd, low, high), jnp.where(is_odd, high, low)


def lat_pack_kernel(fields, lat_a, lat_b):
    row_a = (1 - odd("lat")) * (CY - RIM)
    row_b = odd("lat") * (CY - RIM)
    for f in range(2):
        for x in range(CX):
            at = pl.ds((f * CX + x) * RIM, RIM)
            lat_a[at, :] = fields[f, x, pl.ds(row_a, RIM), :]
            lat_b[at, :] = fields[f, x, pl.ds(row_b, RIM), :]


def lat_pack(fields):
    rows = jax.ShapeDtypeStruct((2 * CX * RIM, NZ), jnp.float32)
    return pl.pallas_call(
        lat_pack_kernel,
        out_shape=[rows, rows],
        in_specs=[VMEM],
        out_specs=[VMEM] * 2,
        compiler_params=params(4),
    )(fields)


def corner_at(f, side, k):
    return pl.ds(((f * 2 + side) * HALO + k) * RIM, RIM)


def corner_pack_kernel(depth_a, depth_b, swept, corner_a, corner_b):
    del swept
    side_a = 1 - odd("depth")
    side_b = odd("depth")
    row_a = (1 - odd("lat")) * (CY - RIM)
    row_b = odd("lat") * (CY - RIM)
    for f in range(2):
        for k in range(HALO):
            for side, halo in ((side_a, depth_a), (side_b, depth_b)):
                corner_a[corner_at(f, side, k), :] = halo[f, k, pl.ds(row_a, RIM), :]
                corner_b[corner_at(f, side, k), :] = halo[f, k, pl.ds(row_b, RIM), :]


def corner_pack(depth_a, depth_b, swept):
    rows = jax.ShapeDtypeStruct((2 * 2 * HALO * RIM, NZ), jnp.float32)
    return pl.pallas_call(
        corner_pack_kernel,
        out_shape=[rows, rows],
        in_specs=[VMEM] * 3,
        out_specs=[VMEM] * 2,
        compiler_params=params(4),
    )(depth_a, depth_b, swept)


def lat_unpack(ext, lat_a, lat_b, corner_a, corner_b):
    row_a = ROW0 - RIM + (1 - odd("lat")) * (RIM + CY)
    row_b = ROW0 - RIM + odd("lat") * (RIM + CY)
    for f in range(2):
        for row, lat, corner in ((row_a, lat_a, corner_a), (row_b, lat_b, corner_b)):
            for x in range(CX):
                at = pl.ds((f * CX + x) * RIM, RIM)
                ext[f, HALO + x, pl.ds(row, RIM), :] = lat[at, :]
            for side in range(2):
                for k in range(HALO):
                    layer = side * (HALO + CX) + k
                    ext[f, layer, pl.ds(row, RIM), :] = corner[corner_at(f, side, k), :]


def zero_layers(ref, first, last):
    depth = lax.axis_index("depth")

    @pl.when(depth == 0)
    def _():
        for f in range(2):
            for x in range(first, HALO):
                ref[f, x] = jnp.zeros((EY, NZ), jnp.float32)

    @pl.when(depth == lax.axis_size("depth") - 1)
    def _():
        for f in range(2):
            for x in range(HALO + CX, last):
                ref[f, x] = jnp.zeros((EY, NZ), jnp.float32)


def zero_rows(ref, first, last):
    lat = lax.axis_index("lat")

    def rows(row):
        def layer(x, carry):
            for f in range(2):
                ref[f, x, pl.ds(row, 8), :] = jnp.zeros((8, NZ), jnp.float32)
            return carry

        lax.fori_loop(first, last, layer, 0, unroll=2)

    @pl.when(lat == 0)
    def _():
        rows(0)

    @pl.when(lat == lax.axis_size("lat") - 1)
    def _():
        rows(ROW0 + CY)


def sweep(j, inp, out, source, first, last, rows, unroll):
    theta = thetas(SWEEPS)
    lane = lax.broadcasted_iota(jnp.int32, (8, NZ), 1)
    low_edge = lane == 0
    high_edge = lane == NZ - 1

    def layer(x, carry):
        for row in rows:
            centres = [inp[f, x, pl.ds(row, 8), :] for f in range(2)]
            if j == 0:
                p, h = centres
                reaction = TIME_STEP * (p * (1.0 - p) * ((p - 0.5) + COUPLE * h))
                sources = (
                    (p + reaction) * (1.0 / DIFFUSION[0]),
                    (h + LATENT * reaction) * (1.0 / DIFFUSION[1]),
                )
                for f in range(2):
                    source[f, x, pl.ds(row, 8), :] = sources[f]
            else:
                sources = [source[f, x, pl.ds(row, 8), :] for f in range(2)]
            for f in range(2):
                u = centres[f]
                around = inp[f, x - 1, pl.ds(row, 8), :] + inp[f, x + 1, pl.ds(row, 8), :]
                sides = inp[f, x, pl.ds(row - 1, 8), :] + inp[f, x, pl.ds(row + 1, 8), :]
                below = jnp.where(low_edge, 0.0, pltpu.roll(u, 1, 1))
                above = jnp.where(high_edge, 0.0, pltpu.roll(u, NZ - 1, 1))
                total = (around + sides) + ((below + above) + sources[f])
                k = DIFFUSION[f]
                inverse = 1.0 / theta[f, j]
                value = float(k * inverse) * total
                own = float(1.0 - (1.0 + 6.0 * k) * inverse)
                if 2 * j + 1 != SWEEPS:
                    value = value + own * u
                out[f, x, pl.ds(row, 8), :] = value
        return carry

    lax.fori_loop(first, last, layer, 0, unroll=unroll)


def first_kernel(fields, packed, ext, once, source, twice, thrice):
    del packed
    for f in range(2):

        def layer(x, carry):
            ext[f, HALO + x, pl.ds(ROW0, CY), :] = fields[f, x]
            return carry

        lax.fori_loop(0, CX, layer, 0, unroll=8)
    sweep(0, ext, once, source, HALO + 1, HALO + CX - 1, INNER, 5)
    sweep(1, once, twice, source, HALO + 2, HALO + CX - 2, INNER, 14)
    sweep(2, twice, thrice, source, HALO + 3, HALO + CX - 3, INNER, 13)


def first(fields, packed):
    return pl.pallas_call(
        first_kernel,
        out_shape=[FIELD] * 5,
        in_specs=[VMEM] * 2,
        out_specs=[VMEM] * 5,
        compiler_params=params(4),
    )(fields, packed)


def inner_kernel(*refs):
    depth_a, depth_b, unused_corner, count = refs[5:9]
    ext, once, source, twice, thrice, pic = refs[9:]
    layer_a = (1 - odd("depth")) * (HALO + CX)
    layer_b = odd("depth") * (HALO + CX)
    for f in range(2):
        for k in range(HALO):
            ext[f, layer_a + k, pl.ds(ROW0, CY), :] = depth_a[f, k]
            ext[f, layer_b + k, pl.ds(ROW0, CY), :] = depth_b[f, k]
    zero_layers(ext, 0, EX)
    for j, (inp, out) in enumerate(((ext, once), (once, twice), (twice, thrice))):
        for start in (1 + j, HALO + CX - 1 - j):
            sweep(j, inp, out, source, start, start + 3, INNER, 3)
        if j < 2:
            zero_layers(out, 1 + j, EX - 1 - j)
    render(INNER_TILES, 4, thrice, count[0, 0], pic)


def inner(fields, halos, corner_a, iface_count):
    return pl.pallas_call(
        inner_kernel,
        out_shape=[FIELD] * 5 + [PICTURES],
        in_specs=[VMEM] * 8 + [SMEM],
        out_specs=[VMEM] * 6,
        input_output_aliases={i: i for i in range(5)},
        compiler_params=params(4),
        cost_estimate=pl.CostEstimate(
            flops=40_000_000, bytes_accessed=1 << 20, transcendentals=0
        ),
    )(*fields, *halos, corner_a, iface_count)


CENTRE = 0.8
SHRINK = 0.5 / CENTRE


def whole_part(v, x):
    base = [math.floor(SHEAR_Y[v] * i / CX) for i in range(CX)]
    value = jnp.int32(base[0])
    for i in range(1, CX):
        if base[i] != base[i - 1]:
            value = value + jnp.where(x >= i, base[i] - base[i - 1], 0)
    return value


def render(tiles, at_once, field, count, pic):
    lane = lax.broadcasted_iota(jnp.int32, (8, NZ), 1)
    scale = -4.0 / NX * math.log2(math.e)
    for v in range(VIEWS):
        for c in range(4):
            for t in tiles:
                pic[v, c, pl.ds(t, 8), :] = jnp.full((8, NZ), 1.0 if c == 3 else 0.0)

    def layers(i, carry):
        for v in range(VIEWS):
            positive = SHEAR_Z[v] > 0
            shift = NZ - 1 if positive else 1
            edge = (lane == NZ - 1) if positive else (lane == 0)
            places = []
            for q in range(at_once):
                x = i * at_once + q
                xf = x.astype(jnp.float32)
                base_y = whole_part(v, x)
                frac_y = xf * (SHEAR_Y[v] / CX) - base_y.astype(jnp.float32)
                frac_z = xf * (abs(SHEAR_Z[v]) / CX)
                own = (1.0 - frac_y) * (1.0 - frac_z)
                ratio = jnp.full((8, NZ), frac_y) / (1.0 - frac_y)
                side = jnp.where(edge, 0.0, jnp.full((8, NZ), frac_z) / (1.0 - frac_z))
                live = jnp.where(x < count, scale * own * own, 0.0)
                places.append((x, base_y, ratio, side, live, own * SHRINK))
            for t in tiles:
                at = pl.ds(t, 8)
                colours = [pic[v, c, at, :] for c in range(3)]
                trans = pic[v, 3, at, :]
                for x, base_y, ratio, side, live, own in places:
                    samples = []
                    for f in range(2):
                        row = ROW0 + t + base_y
                        near = field[f, HALO + x, pl.ds(row, 8), :]
                        far = field[f, HALO + x, pl.ds(row + 1, 8), :]
                        mixed = near + far * ratio
                        samples.append(mixed + pltpu.roll(mixed, shift, 1) * side)
                    passed = trans * jnp.exp2(samples[0] * samples[0] * live)
                    weight = trans - passed
                    trans = passed
                    p = samples[1] * own
                    square = p * p
                    outer = square + (1.0 + CENTRE * CENTRE) * SHRINK * SHRINK
                    colours[0] = colours[0] + weight / (outer + p)
                    colours[1] = colours[1] + weight / (square + SHRINK * SHRINK)
                    colours[2] = colours[2] + weight / (outer - p)
                for c in range(3):
                    pic[v, c, at, :] = colours[c]
                pic[v, 3, at, :] = trans
        return carry

    lax.fori_loop(0, lax.div(count + (at_once - 1), at_once), layers, 0)


def brick_kernel(*refs):
    count = refs[10]
    keep, send, ext, once, source, twice, thrice, pic, turned = refs[11:]
    lat_unpack(ext, *refs[6:10])
    zero_layers(ext, 0, EX)
    zero_rows(ext, 0, EX)
    sweep(0, ext, once, source, 1, EX - 1, STRIPS, 12)
    zero_layers(once, 1, EX - 1)
    zero_rows(once, 1, EX - 1)
    sweep(1, once, twice, source, 2, EX - 2, STRIPS, 17)
    zero_layers(twice, 2, EX - 2)
    zero_rows(twice, 2, EX - 2)
    sweep(2, twice, thrice, source, HALO, HALO + CX, STRIPS, 16)
    zero_rows(thrice, HALO, HALO + CX)
    render(OUTER_TILES, 8, thrice, count[0, 0], pic)
    for v in range(2):
        for c in range(4):
            square = jnp.concatenate([pic[v, c], pltpu.roll(pic[3 - v, c], 64, 1)], axis=0)
            if c < 3:
                square = square * (SHRINK * SHRINK)
            turned[v, c] = square.T
    depth = lax.axis_index("depth")
    my_core = lax.rem(depth, 2)
    my_x = lax.rem(lax.div(depth, 2), 4)
    for core_rel, target in ((0, keep), (1, send)):
        for x_rel in range(4):
            block = (my_x ^ x_rel) * 2 + (my_core ^ core_rel)
            for z in range(4):
                at = pl.ds(pl.multiple_of((block + (z & 1) * 8) * 8, 8), 8)
                for c in range(4):
                    target[x_rel * 4 + z, c] = turned[z >> 1, c, at, :]


def brick(fields, rims, iface_count):
    pieces = jax.ShapeDtypeStruct((16, 4, 8, NZ), jnp.float32)
    results = pl.pallas_call(
        brick_kernel,
        out_shape=[pieces, pieces] + [FIELD] * 5 + [PICTURES],
        in_specs=[VMEM] * 10 + [SMEM],
        out_specs=[VMEM] * 8,
        input_output_aliases={i: 2 + i for i in range(6)},
        scratch_shapes=[pltpu.VMEM((2, 4, NZ, 2 * CY), jnp.float32)],
        compiler_params=params(4),
    )(*fields, *rims, iface_count)
    return results[0], results[1], results[6]


def emit_kernel(field, part, phase_next, heat_next, token, sems):
    copies = []
    for f, target in enumerate((phase_next, heat_next)):
        copies.append(
            pltpu.make_async_copy(
                field.at[f, pl.ds(HALO, CX), pl.ds(ROW0, CY), :], target, sems.at[f]
            )
        )
        copies[f].start()
    token[...] = part[0, 0]
    for copy in copies:
        copy.wait()


def emit(field, part):
    block = jax.ShapeDtypeStruct((CX, CY, NZ), jnp.float32)
    return pl.pallas_call(
        emit_kernel,
        out_shape=[block, block, jax.ShapeDtypeStruct((8, NZ), jnp.float32)],
        in_specs=[VMEM, VMEM],
        out_specs=[HBM, HBM, VMEM],
        scratch_shapes=[pltpu.SemaphoreType.DMA((2,))],
        compiler_params=params(4),
    )(field, part)


def blend(front, back, write):
    clear = front[:, 3]
    for c in range(3):
        write(c, front[:, c] + clear * back[:, c])
    write(3, clear * back[:, 3])


def core_kernel(mine, theirs, token, *parts):
    del token
    in_front = lax.rem(lax.axis_index("depth"), 2) == 0

    def write(c, value):
        for i, part in enumerate(parts):
            part[:, c] = value[4 * i : 4 * i + 4]

    @pl.when(in_front)
    def _():
        blend(mine, theirs, write)

    @pl.when(jnp.logical_not(in_front))
    def _():
        blend(theirs, mine, write)


def core_combine(mine, theirs, token):
    part = jax.ShapeDtypeStruct((4,) + mine.shape[1:], jnp.float32)
    return pl.pallas_call(
        core_kernel,
        out_shape=[part] * 4,
        in_specs=[VMEM] * 3,
        out_specs=[VMEM] * 4,
        compiler_params=params(4),
    )(mine, theirs, token)


def x_kernel(*refs):
    parts, out = refs[:4], refs[4]
    my_x = lax.rem(lax.div(lax.axis_index("depth"), 2), 4)
    low = lax.broadcasted_iota(jnp.int32, (8, NZ), 1) < CY

    def ordered(place):
        for z in range(4):
            back = parts[3 ^ place]
            total = [back[z, c] for c in range(4)]
            for x in (2, 1, 0):
                front = parts[x ^ place]
                clear = front[z, 3]
                total = [front[z, c] + clear * total[c] for c in range(3)] + [clear * total[3]]
            for pair in range(2):
                a, b = total[2 * pair], total[2 * pair + 1]
                out[z, pair] = jnp.where(low, a, pltpu.roll(b, CY, 1))
                out[7 - z, pair] = jnp.where(low, pltpu.roll(a, CY, 1), b)

    for place in range(4):
        pl.when(my_x == place)(functools.partial(ordered, place))


def x_combine(parts):
    return pl.pallas_call(
        x_kernel,
        out_shape=jax.ShapeDtypeStruct((8, 2, 8, NZ), jnp.float32),
        in_specs=[VMEM] * 4,
        out_specs=VMEM,
        compiler_params=params(4),
    )(*parts)


def z_kernel(slabs, out):
    low = lax.broadcasted_iota(jnp.int32, (8, NZ), 1) < CY
    first_pair, second_pair = slabs[7, 0], slabs[7, 1]
    for z in range(6, -1, -1):
        ahead = slabs[z, 1]
        clear = jnp.where(low, pltpu.roll(ahead, CY, 1), ahead)
        first_pair = slabs[z, 0] + clear * first_pair
        second_pair = jnp.where(low, ahead, 0.0) + clear * second_pair
    out[0] = first_pair[:, :CY]
    out[1] = first_pair[:, CY:]
    out[2] = second_pair[:, :CY]
    out[3] = second_pair[:, CY:]


def z_combine(slabs):
    return pl.pallas_call(
        z_kernel,
        out_shape=jax.ShapeDtypeStruct((4, 8, CY), jnp.float32),
        in_specs=[VMEM],
        out_specs=VMEM,
        compiler_params=params(4),
    )(slabs).transpose(0, 2, 1)


def pairs(count, start):
    result = []
    for i in range(start, count, 2):
        after = (i + 1) % count
        result += [(i, after), (after, i)]
    return result


def per_device(phase, temper, iface_count):
    depth_size = lax.axis_size("depth")
    lat_size = lax.axis_size("lat")
    depth_pairs = [pairs(depth_size, start) for start in range(2)]
    lat_pairs = [pairs(lat_size, start) for start in range(2)]
    fields = jnp.stack([phase, temper])
    halos = depth_pack(fields)
    halos = [lax.ppermute(h, "depth", p) for h, p in zip(halos, depth_pairs)]
    packed = lat_pack(fields)
    rims = [lax.ppermute(h, "lat", p) for h, p in zip(packed, lat_pairs)]
    fields = first(fields, packed[0])
    packed = corner_pack(*halos, fields[1])
    corners = [lax.ppermute(h, "lat", p) for h, p in zip(packed, lat_pairs)]
    fields = inner(fields, halos, packed[0], iface_count)
    mine, outgoing, solved = brick(fields, (*rims, *corners), iface_count)

    def partner(value, distance):
        return lax.ppermute(value, "depth", [(i, i ^ distance) for i in range(depth_size)])

    theirs = partner(outgoing, 1)
    phase_next, heat_next, token = emit(solved, mine)
    parts = core_combine(mine, theirs, token)
    parts = [parts[0]] + [partner(parts[k], 2 * k) for k in (1, 2, 3)]
    groups = [[z * 8 + i for z in range(depth_size // 8)] for i in range(8)]
    slabs = lax.all_to_all(
        x_combine(parts), "depth", 0, 0, tiled=True, axis_index_groups=groups
    )
    return phase_next, heat_next, z_combine(slabs)


def solution(mesh):
    return jax.shard_map(
        per_device,
        mesh=mesh,
        in_specs=(P("depth", "lat", None), P("depth", "lat", None), P("depth", "lat")),
        out_specs=(P("depth", "lat", None), P("depth", "lat", None), P(None, "lat", "depth")),
        check_vma=False,
    )
```
